256 devices in a mesh: dp: 16 (over z_hi, y, core), space: 16 (over x, z_lo).
Axes of the slice: x: 4, y: 4, z: 8 (z_hi: 2, z_lo: 4; z = z_hi * 4 + z_lo), core: 2. Of those that a mesh axis runs over, the one named last changes fastest.
Arguments:
- fields: bfloat16 [16, 128, 128, 512], P('dp', 'space'), may hold values from -6 to 6
- bn_scale: float32 [512], replicated, may hold values from 0.5 to 1.5
- bn_shift: float32 [512], replicated, may hold values from -3 to 3
- w_expand: bfloat16 [512, 2048], P(None, 'dp'), may hold values from -0.25 to 0.25
- expand_bias: float32 [2048], replicated, may hold values from -3 to 3
- dw_kernel: float32 [3, 3, 2048], replicated, may hold values from -2 to 2
- dw_bias: float32 [2048], replicated, may hold values from -3 to 3
- w_project: bfloat16 [2048, 512], P(None, 'dp'), may hold values from -0.125 to 0.125
- ln_gain: float32 [512], replicated, may hold values from 0.5 to 1.5
- ln_bias: float32 [512], replicated, may hold values from -3 to 3
- w_qkv: bfloat16 [512, 1536], P(None, 'dp'), may hold values from -0.25 to 0.25
- w_out: bfloat16 [512, 512], P(None, 'dp'), may hold values from -0.25 to 0.25
Outputs:
- output: bfloat16 [16, 128, 128, 512], P('dp', 'space')
The draws below stay inside these ranges and needn't reach their ends.
All inputs are finite; a program needn't handle non-finite values.
Results may differ from the reference program's by a relative error of at most 0.0056.
Values may be sent and summed in bfloat16 or wider, within the bound.
A program may use at most 64 MiB of HBM per device.

```python
import jax
import jax.numpy as jnp
from jax import lax

C = 512
FF = 2048
HD = 32
GRID = 8
HEIGHT = 128
COLS = 128
SAMPLES = 16


def block_levels(own_key, extent, shards, low, largest):
    factor_of, own = 1.0, jax.random.fold_in(own_key, 6)
    for axis_at, shards_of in shards:
        draws = jnp.exp(jax.random.uniform(jax.random.fold_in(own, axis_at), (shards_of,), jnp.float32, low / len(shards), largest / len(shards)))
        factor_of = factor_of * jnp.repeat(draws, extent[axis_at] // shards_of).reshape([-1 if axis == axis_at else 1 for axis in range(len(extent))])
    return factor_of


def normal_values(rng, shape, scale, reach, shards=(), dtype=jnp.bfloat16):
    array = jax.random.normal(rng, shape, jnp.float32) * scale
    if len(shards) > 0:
        array = block_levels(rng, shape, shards, -0.22, 0.18) * array
    return jnp.clip(array, min=-reach, max=reach).astype(dtype)


def setup_inputs(seed: int = 0) -> dict:
    arg_keys = jax.random.split(jax.random.key(seed), 13)
    return {
        "fields": normal_values(arg_keys[0], (SAMPLES, HEIGHT, COLS, C), 1.0, 6.0, ((0, 16), (1, 16))),
        "bn_scale": jnp.clip(1.0 + 0.1 * jax.random.normal(arg_keys[1], (C,), jnp.float32), 0.5, 1.5),
        "bn_shift": normal_values(arg_keys[2], (C,), 0.5, 3.0, (), jnp.float32),
        "w_expand": normal_values(arg_keys[3], (C, FF), C ** -0.5, 0.25, ((1, 16),)),
        "expand_bias": normal_values(arg_keys[4], (FF,), 0.5, 3.0, (), jnp.float32),
        "dw_kernel": normal_values(arg_keys[5], (3, 3, FF), 9 ** -0.5, 2.0, (), jnp.float32),
        "dw_bias": normal_values(arg_keys[6], (FF,), 0.5, 3.0, (), jnp.float32),
        "w_project": normal_values(arg_keys[7], (FF, C), FF ** -0.5, 0.125, ((1, 16),)),
        "ln_gain": jnp.clip(1.0 + 0.1 * jax.random.normal(arg_keys[8], (C,), jnp.float32), 0.5, 1.5),
        "ln_bias": normal_values(arg_keys[9], (C,), 0.4, 3.0, (), jnp.float32),
        "w_qkv": normal_values(arg_keys[10], (C, 3 * C), C ** -0.5, 0.25, ((1, 16),)),
        "w_out": normal_values(arg_keys[11], (C, C), C ** -0.5, 0.25, ((1, 16),)),
    }


def layer_normed(tokens, ln_gain, ln_bias):
    values = tokens.astype(jnp.float32)
    center = lax.optimization_barrier(jnp.mean(values, axis=-1, keepdims=True))
    spread = lax.optimization_barrier(jnp.mean(jnp.square(values - center), axis=-1, keepdims=True))
    return ((values - center) * lax.rsqrt(spread + 1e-05) * ln_gain + ln_bias).astype(jnp.bfloat16)

def attend_windows(queries, keyset, valueset):
    window_count, length, width = queries.shape
    heads = width // HD
    query_heads = queries.reshape(window_count, length, heads, HD).astype(jnp.float32)
    key_heads = keyset.reshape(window_count, length, heads, HD).astype(jnp.float32)
    value_heads = valueset.reshape(window_count, length, heads, HD).astype(jnp.float32)
    scores = jnp.einsum('wqhd,wkhd->whqk', query_heads, key_heads) / jnp.sqrt(jnp.float32(HD))
    exponent = jnp.exp(scores)
    soft_weights = (exponent / lax.optimization_barrier(jnp.sum(exponent, axis=-1, keepdims=True))).astype(jnp.bfloat16)
    mixed = jnp.einsum('whqk,wkhd->wqhd', soft_weights.astype(jnp.float32), value_heads)
    return mixed.astype(jnp.bfloat16).reshape(window_count, length, width)

def reference(fields, bn_scale, bn_shift, w_expand, expand_bias, dw_kernel, dw_bias, w_project, ln_gain, ln_bias, w_qkv, w_out):
    stride_rows = HEIGHT // GRID
    stride_cols = COLS // GRID

    def one_sample(sample):
        normed = (sample.astype(jnp.float32) * bn_scale + bn_shift).astype(jnp.bfloat16)
        expanded = jax.nn.gelu(jnp.dot(normed.reshape(-1, C), w_expand, preferred_element_type=jnp.float32) + expand_bias)
        expanded = expanded.astype(jnp.bfloat16).reshape(HEIGHT, COLS, FF)
        padded = jnp.pad(expanded, ((1, 1), (1, 1), (0, 0)))
        accum = jnp.zeros((HEIGHT, COLS, FF), jnp.float32)
        for row_off in range(3):
            for col_off in range(3):
                accum = accum + padded[row_off:row_off + HEIGHT, col_off:col_off + COLS].astype(jnp.float32) * dw_kernel[row_off, col_off]
        spatial = jax.nn.gelu(accum + dw_bias).astype(jnp.bfloat16)
        projected = jnp.dot(spatial.reshape(-1, FF), w_project, preferred_element_type=jnp.float32)
        conv_out = (sample.astype(jnp.float32) + projected.reshape(HEIGHT, COLS, C)).astype(jnp.bfloat16)
        normal_two = layer_normed(conv_out, ln_gain, ln_bias)
        triple = jnp.dot(normal_two.reshape(-1, C), w_qkv, preferred_element_type=jnp.float32).astype(jnp.bfloat16)
        grouped = triple.reshape(GRID, stride_rows, GRID, stride_cols, 3 * C).transpose(1, 3, 0, 2, 4)
        grouped = grouped.reshape(stride_rows * stride_cols, GRID * GRID, 3 * C)
        attended = attend_windows(grouped[..., :C], grouped[..., C:2 * C], grouped[..., 2 * C:])
        restored = attended.reshape(stride_rows, stride_cols, GRID, GRID, C).transpose(2, 0, 3, 1, 4).reshape(HEIGHT * COLS, C)
        final = conv_out.astype(jnp.float32) + jnp.dot(restored, w_out, preferred_element_type=jnp.float32).reshape(HEIGHT, COLS, C)
        return final.astype(jnp.bfloat16)
    return lax.map(one_sample, fields)
```

```python
import jax
import jax.numpy as jnp
from jax import lax
from jax.experimental import pallas as pl
from jax.experimental.pallas import tpu as pltpu
from jax.sharding import PartitionSpec as P

F32 = jnp.float32
BF16 = jnp.bfloat16
NY, NX, NZ = 4, 4, 4
ROWS, COLS, CH, FF = 8, 128, 512, 2048
Q_SCALE = 1.4426950408889634 / (32.0**0.5)


def dot_nn(a, b):
    return jnp.dot(a, b, preferred_element_type=F32)


def dot_nt(a, b):
    return lax.dot_general(a, b, (((1,), (1,)), ((), ())), preferred_element_type=F32)


def gelu(x):
    inner = x * (0.7978845608028654 + 0.035677408136300125 * (x * x))
    half = 0.5 * x
    return half + half * jnp.tanh(inner)


def eye(n):
    return (
        lax.broadcasted_iota(jnp.int32, (n, n), 0) == lax.broadcasted_iota(jnp.int32, (n, n), 1)
    ).astype(BF16)


def kernel(
    f_ref, bns_ref, bnb_ref, wex_ref, be_ref, dwk_ref, dwb_ref, wpr_ref, lng_ref, lnb_ref, wqkv_ref, wout_ref,
    o_ref,
    halo, fperm, xn, we, w1, w2, ebuf, sbuf, co, gbuf, qkv, fin, rbuf,
    wsend, wrecv, hsend, hrecv, asend, arecv, rsend, rrecv,
):
    dp = lax.axis_index("dp")
    sp = lax.axis_index("space")
    core, yy, zh = dp % 2, (dp // 2) % NY, dp // (2 * NY)
    xx, zl = sp // NZ, sp % NZ
    par, half = zl % 2, zl // 2
    mine = 2 * xx + half

    def at(z_hi, y, c, x, z_lo):
        return {"dp": (z_hi * NY + y) * 2 + c, "space": x * NZ + z_lo}

    y_up, y_dn, y_far = (yy + 1) % NY, (yy + NY - 1) % NY, (yy + 2) % NY
    dev_up = at(zh, y_up, core, xx, zl)
    dev_dn = at(zh, y_dn, core, xx, zl)
    dev_sib = at(zh, yy, 1 - core, xx, zl)
    dev_mir = at(1 - zh, yy, core, xx, NZ - 1 - zl)
    dev_next = {"dp": dp, "space": (sp + 1) % 16}
    dev_prev = {"dp": dp, "space": (sp + 15) % 16}

    def member(k):
        return {"dp": dp, "space": (k // 2) * NZ + (k % 2) * 2 + par}

    barrier = pltpu.get_barrier_semaphore()
    peers = [dev_up, dev_dn, dev_sib, dev_mir, dev_next, dev_prev]
    peers += [member((mine + m) % 8) for m in range(1, 8)]
    for peer in peers:
        pl.semaphore_signal(barrier, inc=1, device_id=peer)
    pl.semaphore_wait(barrier, len(peers))

    pending = []

    def remote(src, dst, send, recv, dev):
        return pltpu.make_async_remote_copy(
            src_ref=src, dst_ref=dst, send_sem=send, recv_sem=recv, device_id=dev
        )

    def push(src, dst, send, recv, dev):
        copy = remote(src, dst, send, recv, dev)
        copy.start()
        pending.append(copy)

    def shard(z_hi, y, c):
        return (z_hi * NY + y) * 2 + c

    bufs = (we, w1, w2)
    own_d = shard(zh, yy, core)
    oth = 1 - zh

    def wpush(ph, slot, d, dev, src=None, lo=None, n=None):
        dst = bufs[ph].at[d] if lo is None else bufs[ph].at[d, pl.ds(lo, n)]
        push(dst if src is None else src, dst, wsend.at[ph, slot], wrecv.at[ph, slot], dev)

    def wwait(ph, slot, d, lo=None, n=None):
        dst = bufs[ph].at[d] if lo is None else bufs[ph].at[d, pl.ds(lo, n)]
        remote(dst, dst, wsend.at[ph, slot], wrecv.at[ph, slot], dev_sib).wait_recv()

    halves = tuple(b.shape[1] // 2 for b in bufs)

    def g_start(ph, src=None):
        wpush(ph, 0, own_d, dev_up, src)
        wpush(ph, 1, own_d, dev_dn, src)
        wpush(ph, 2, own_d, dev_mir, src)
        wpush(ph, 3, own_d, dev_sib, src)

    def g_ring(ph, z_hi, base, sib):
        n = halves[ph]
        up_slot, dn_slot = (0, 1) if base == 4 else (8, 9)
        d_dn, d_up = shard(z_hi, y_dn, core), shard(z_hi, y_up, core)
        wwait(ph, up_slot, d_dn)
        wpush(ph, base, d_dn, dev_up, None, 0, n)
        wwait(ph, dn_slot, d_up)
        wpush(ph, base + 1, d_up, dev_dn, None, n, n)
        wpush(ph, sib, d_dn, dev_sib)
        wpush(ph, sib + 1, d_up, dev_sib)

    def g_ev1(ph):
        g_ring(ph, zh, 4, 6)
        d = shard(oth, yy, core)
        wwait(ph, 2, d)
        wpush(ph, 8, d, dev_up)
        wpush(ph, 9, d, dev_dn)
        wpush(ph, 10, d, dev_sib)

    def g_far(ph, z_hi, base, sib):
        n = halves[ph]
        d = shard(z_hi, y_far, core)
        wwait(ph, base, d, 0, n)
        wwait(ph, base + 1, d, n, n)
        wpush(ph, sib, d, dev_sib)

    def g_ev2(ph):
        g_ring(ph, oth, 11, 13)

    def g_ev3(ph):
        g_far(ph, zh, 4, 15)

    def g_ev4(ph):
        g_far(ph, oth, 11, 16)

    def sib_wait(ph, slot, z_hi, y):
        wwait(ph, slot, shard(z_hi, y, 1 - core))

    def sib_all(ph):
        sib_wait(ph, 3, zh, yy)
        sib_wait(ph, 6, zh, y_dn)
        sib_wait(ph, 7, zh, y_up)
        sib_wait(ph, 10, oth, yy)
        sib_wait(ph, 13, oth, y_dn)
        sib_wait(ph, 14, oth, y_up)
        sib_wait(ph, 15, zh, y_far)
        sib_wait(ph, 16, oth, y_far)

    g_start(0, wex_ref)
    push(f_ref.at[ROWS - 1], halo.at[0], hsend.at[0], hrecv.at[0], dev_next)
    push(f_ref.at[0], halo.at[1], hsend.at[1], hrecv.at[1], dev_prev)

    we[own_d] = wex_ref[...]
    w1[own_d] = dot_nt(eye(32), wpr_ref[...]).astype(BF16)
    w2[own_d, 0:96] = dot_nt(eye(96), wqkv_ref[...]).astype(BF16)
    w2[own_d, 96:128] = dot_nt(eye(32), wout_ref[...]).astype(BF16)

    tok = lax.broadcasted_iota(jnp.int32, (COLS, COLS), 0)
    col = lax.broadcasted_iota(jnp.int32, (COLS, COLS), 1)
    perm = ((tok % 8) * 16 + tok // 8 == col).astype(BF16)
    unperm = ((tok % 16) * 8 + tok // 16 == col).astype(BF16)

    def prep(row, value):
        moved = dot_nn(perm, value)
        xn[row] = (moved * bns_ref[...] + bnb_ref[...]).astype(BF16)
        return moved.astype(BF16)

    @pl.loop(0, ROWS)
    def _(r):
        fperm[r] = prep(r + 1, f_ref[r])

    remote(halo.at[0], halo.at[0], hsend.at[0], hrecv.at[0], dev_next).wait_recv()
    remote(halo.at[1], halo.at[1], hsend.at[1], hrecv.at[1], dev_prev).wait_recv()
    prep(0, halo[0])
    prep(ROWS + 1, halo[1])

    sub = lax.broadcasted_iota(jnp.int32, (2, 8, 128), 1)

    def expand(g):
        @pl.loop(0, (ROWS + 2) // 2)
        def _(r2):
            x = xn[pl.ds(2 * r2, 2)].reshape(2 * COLS, CH)
            w = jnp.concatenate([we[2 * g], we[2 * g + 1]], axis=1)
            bias = be_ref[:, pl.ds(pl.multiple_of(256 * g, 256), 256)]
            e = gelu(dot_nn(x, w) + bias)
            for k in range(2):
                part = e[:, 128 * k : 128 * (k + 1)].reshape(2, 16, 8, 128)
                rows = pl.ds(2 * r2, 2)
                ebuf[2 * g + k, rows, 1:17] = part
                before = pltpu.roll(part[:, 15], 1, 1)
                ebuf[2 * g + k, rows, 0] = jnp.where(sub == 0, 0.0, before)
                after = pltpu.roll(part[:, 0], 7, 1)
                ebuf[2 * g + k, rows, 17] = jnp.where(sub == 7, 0.0, after)

    def pair(z_hi, y):
        return z_hi * NY + y

    sib_wait(0, 3, zh, yy)
    expand(pair(zh, yy))
    g_ev1(0)
    sib_wait(0, 6, zh, y_dn)
    expand(pair(zh, y_dn))
    sib_wait(0, 7, zh, y_up)
    expand(pair(zh, y_up))
    g_ev2(0)
    g_start(1)
    g_ev3(0)
    sib_wait(0, 10, oth, yy)
    expand(pair(oth, yy))
    g_ev4(0)
    sib_wait(0, 15, zh, y_far)
    expand(pair(zh, y_far))
    g_ev1(1)
    sib_wait(0, 13, oth, y_dn)
    expand(pair(oth, y_dn))
    sib_wait(0, 14, oth, y_up)
    expand(pair(oth, y_up))
    g_ev2(1)
    sib_wait(0, 16, oth, y_far)
    expand(pair(oth, y_far))
    g_start(2)
    g_ev3(1)

    @pl.when(sp == 0)
    def _():
        ebuf[:, 0] = jnp.zeros((16, 18, 8, 128), F32)

    @pl.when(sp == 15)
    def _():
        ebuf[:, ROWS + 1] = jnp.zeros((16, 18, 8, 128), F32)

    def conv(q):
        @pl.loop(0, 8)
        def _(g):
            for k in range(2):
                lanes = pl.ds(pl.multiple_of(256 * g + 128 * k, 128), 128)
                taps = dwk_ref[:, lanes]
                bias = dwb_ref[:, lanes]
                for r in range(2):
                    acc = jnp.broadcast_to(bias[None], (16, 8, 128))
                    for i in range(3):
                        for j in range(3):
                            t = 3 * i + j
                            acc = acc + ebuf[2 * g + k, 2 * q + r + i, j : j + 16] * taps[t : t + 1][None]
                    sbuf[g, 128 * r : 128 * (r + 1), 128 * k : 128 * (k + 1)] = (
                        gelu(acc).astype(BF16).reshape(128, 128)
                    )

    def project(q):
        w = w1[...].reshape(CH, FF)
        total = fperm[pl.ds(2 * q, 2)].reshape(2 * COLS, CH).astype(F32)
        for g in range(8):
            total = total + dot_nt(sbuf[g], w[:, 256 * g : 256 * (g + 1)])
        co[pl.ds(2 * q, 2)] = total.astype(BF16).reshape(2, COLS, CH)

    def forward(t, q, u):
        e = half if u == 0 else 1 - half
        push(
            co.at[2 * q + e], gbuf.at[mine], asend.at[2 * t + u], arecv.at[2 * t + u], member(2 * q + e)
        )

    def arrived(t, u):
        e = half if u == 0 else 1 - half
        src = 2 * ((xx + 3 - t) % NX) + e
        remote(
            gbuf.at[src], gbuf.at[src], asend.at[2 * t + u], arecv.at[2 * t + u], member(src)
        ).wait_recv()

    for t in range(4):
        q = (xx + 1 + t) % NX
        conv(q)
        if t == 0:
            g_ev4(1)
            sib_all(1)
        project(q)
        if t < 3:
            forward(t, q, 1)
            forward(t, q, 0)
        else:
            forward(t, q, 1)
            gbuf[mine] = co[mine]
        if t == 0:
            g_ev1(2)
        if t == 1:
            g_ev2(2)
            g_ev3(2)
        if t == 2:
            g_ev4(2)
    sib_all(2)

    def tokens_of(i2):
        values = gbuf[pl.ds(2 * i2, 2)].reshape(2 * COLS, CH).astype(F32)
        center = jnp.mean(values, axis=-1, keepdims=True)
        off = values - center
        spread = jnp.mean(off * off, axis=-1, keepdims=True)
        ln = (off * lax.rsqrt(spread + 1e-05) * lng_ref[...] + lnb_ref[...]).astype(BF16)
        w = w2[:, 0:96].reshape(3 * CH, CH)
        rows = pl.ds(2 * i2, 2)
        qkv[rows, :, 0:CH] = (dot_nt(ln, w[0:CH]) * Q_SCALE).astype(BF16).reshape(2, COLS, CH)
        qkv[rows, :, CH : 2 * CH] = dot_nt(ln, w[CH : 2 * CH]).astype(BF16).reshape(2, COLS, CH)
        qkv[rows, :, 2 * CH :] = dot_nt(ln, w[2 * CH :]).astype(BF16).reshape(2, COLS, CH)

    for t in range(4):
        if t < 3:
            arrived(t, 0)
        arrived(t, 1)
        tokens_of((xx + 3 - t) % NX)

    lane = lax.broadcasted_iota(jnp.int32, (128, 128), 1)
    row = lax.broadcasted_iota(jnp.int32, (128, 128), 0)
    heads = [(lane // 32 == n) for n in range(4)]
    same = (lane // 8) % 2 == (row // 8) % 2
    same4 = jnp.concatenate([same] * 4, axis=0)

    def windows(bp):
        rows = pl.ds(pl.multiple_of(16 * bp, 16), 16)
        parts = []
        for gr in range(4):
            lo = 128 * gr
            qv = qkv[:, rows, lo : lo + 128].reshape(128, 128)
            kv = qkv[:, rows, CH + lo : CH + lo + 128].reshape(128, 128)
            vv = qkv[:, rows, 2 * CH + lo : 2 * CH + lo + 128].reshape(128, 128)
            zero = jnp.zeros_like(qv)
            qm = jnp.concatenate([jnp.where(m, qv, zero) for m in heads], axis=0)
            vm = jnp.concatenate([jnp.where(m, vv, zero) for m in heads], axis=0)
            e = jnp.where(same4, jnp.exp2(dot_nt(qm, kv)), 0.0)
            p = (e * (1.0 / jnp.sum(e, axis=1, keepdims=True))).astype(BF16)
            wide = jnp.concatenate([p[128 * n : 128 * (n + 1)] for n in range(4)], axis=1)
            parts.append(dot_nn(wide, vm).astype(BF16))
        return jnp.concatenate(parts, axis=1)

    for c in range(4):
        @pl.loop(2 * c, 2 * c + 2)
        def _(bp):
            rows = pl.ds(pl.multiple_of(16 * bp, 16), 16)
            wo = w2[:, 96:128].reshape(CH, CH)
            done = dot_nt(windows(bp), wo) + gbuf[:, rows].reshape(128, CH).astype(F32)
            fin[:, rows] = done.astype(BF16).reshape(8, 16, CH)

        span = pl.ds(32 * c, 32)
        for m in range(1, 8):
            k = (mine + m) % 8
            push(
                fin.at[k, span], rbuf.at[mine, span], rsend.at[c, m - 1], rrecv.at[c, m - 1], member(k)
            )

    o_ref[mine] = dot_nn(unperm, fin[mine]).astype(BF16)
    for m in range(1, 8):
        k = (mine + 8 - m) % 8
        for c in range(4):
            span = pl.ds(32 * c, 32)
            remote(
                rbuf.at[k, span], rbuf.at[k, span], rsend.at[c, m - 1], rrecv.at[c, m - 1], member(k)
            ).wait_recv()
        o_ref[k] = dot_nn(unperm, rbuf[k]).astype(BF16)

    for copy in pending:
        copy.wait_send()


def local(
    fields, bn_scale, bn_shift, w_expand, expand_bias, dw_kernel, dw_bias, w_project, ln_gain, ln_bias, w_qkv, w_out
):
    vmem = pl.BlockSpec(memory_space=pltpu.VMEM)
    dma = pltpu.SemaphoreType.DMA
    out = pl.pallas_call(
        kernel,
        out_shape=jax.ShapeDtypeStruct((ROWS, COLS, CH), BF16),
        in_specs=[vmem] * 12,
        out_specs=vmem,
        scratch_shapes=[
            pltpu.VMEM((2, COLS, CH), BF16),
            pltpu.VMEM((ROWS, COLS, CH), BF16),
            pltpu.VMEM((ROWS + 2, COLS, CH), BF16),
            pltpu.VMEM((16, CH, 128), BF16),
            pltpu.VMEM((16, 32, FF), BF16),
            pltpu.VMEM((16, 128, CH), BF16),
            pltpu.VMEM((16, ROWS + 2, 18, 8, 128), F32),
            pltpu.VMEM((8, 256, 256), BF16),
            pltpu.VMEM((ROWS, COLS, CH), BF16),
            pltpu.VMEM((ROWS, COLS, CH), BF16),
            pltpu.VMEM((ROWS, COLS, 3 * CH), BF16),
            pltpu.VMEM((ROWS, COLS, CH), BF16),
            pltpu.VMEM((ROWS, COLS, CH), BF16),
            dma((3, 17)),
            dma((3, 17)),
            dma((2,)),
            dma((2,)),
            dma((8,)),
            dma((8,)),
            dma((4, 7)),
            dma((4, 7)),
        ],
        compiler_params=pltpu.CompilerParams(
            collective_id=0, has_side_effects=True, vmem_limit_bytes=60 * 1024 * 1024
        ),
    )(
        fields.reshape(ROWS, COLS, CH),
        bn_scale.reshape(1, CH),
        bn_shift.reshape(1, CH),
        w_expand,
        expand_bias.reshape(1, FF),
        dw_kernel.reshape(9, FF),
        dw_bias.reshape(1, FF),
        w_project,
        ln_gain.reshape(1, CH),
        ln_bias.reshape(1, CH),
        w_qkv,
        w_out,
    )
    return out.reshape(fields.shape)


def solution(mesh):
    in_specs = (
        P("dp", "space", None, None),
        P(),
        P(),
        P(None, "dp"),
        P(),
        P(),
        P(),
        P(None, "dp"),
        P(),
        P(),
        P(None, "dp"),
        P(None, "dp"),
    )
    out_specs = P("dp", "space", None, None)
    return jax.shard_map(local, mesh=mesh, in_specs=in_specs, out_specs=out_specs, check_vma=False)
```

```python
import jax
import jax.numpy as jnp
from jax import lax
from jax.experimental import pallas as pl
from jax.experimental.pallas import tpu as pltpu
from jax.sharding import PartitionSpec as P

F32 = jnp.float32
BF16 = jnp.bfloat16
NY, NX, NZ = 4, 4, 4
ROWS, COLS, CH, FF = 8, 128, 512, 2048
Q_SCALE = 1.4426950408889634 / (32.0**0.5)


def dot_nn(a, b):
    return jnp.dot(a, b, preferred_element_type=F32)


def dot_nt(a, b):
    return lax.dot_general(a, b, (((1,), (1,)), ((), ())), preferred_element_type=F32)


def gelu(x):
    inner = x * (0.7978845608028654 + 0.035677408136300125 * (x * x))
    half = 0.5 * x
    return half + half * jnp.tanh(inner)


def kernel(
    f_ref, bns_ref, bnb_ref, wex_ref, be_ref, dwk_ref, dwb_ref, wpr_ref, lng_ref, lnb_ref, wqkv_ref, wout_ref,
    o_ref,
    fbuf, halo, fperm, xn, we, w1, w2, ebuf, sbuf, co, gbuf, qkv, fin,
    lsem, wsend, wrecv, hsend, hrecv, asend, arecv, rsend, rrecv,
):
    dp = lax.axis_index("dp")
    sp = lax.axis_index("space")
    core, yy, zh = dp % 2, (dp // 2) % NY, dp // (2 * NY)
    xx, zl = sp // NZ, sp % NZ
    par, half = zl % 2, zl // 2
    mine = 2 * xx + half

    def at(z_hi, y, c, x, z_lo):
        return {"dp": (z_hi * NY + y) * 2 + c, "space": x * NZ + z_lo}

    y_up, y_dn, y_far = (yy + 1) % NY, (yy + NY - 1) % NY, (yy + 2) % NY
    dev_up = at(zh, y_up, core, xx, zl)
    dev_dn = at(zh, y_dn, core, xx, zl)
    dev_far = at(zh, y_far, core, xx, zl)
    dev_sib = at(zh, yy, 1 - core, xx, zl)
    dev_mir = at(1 - zh, yy, core, xx, NZ - 1 - zl)
    dev_xup = at(zh, yy, core, (xx + 1) % NX, zl)
    dev_xdn = at(zh, yy, core, (xx + NX - 1) % NX, zl)
    dev_next = {"dp": dp, "space": (sp + 1) % 16}
    dev_prev = {"dp": dp, "space": (sp + 15) % 16}

    def member(k):
        return {"dp": dp, "space": (k // 2) * NZ + (k % 2) * 2 + par}

    barrier = pltpu.get_barrier_semaphore()
    peers = [dev_up, dev_dn, dev_far, dev_sib, dev_mir, dev_next, dev_prev]
    peers += [member((mine + m) % 8) for m in range(1, 8)]
    for peer in peers:
        pl.semaphore_signal(barrier, inc=1, device_id=peer)

    pending = []

    def remote(src, dst, send, recv, dev):
        return pltpu.make_async_remote_copy(
            src_ref=src, dst_ref=dst, send_sem=send, recv_sem=recv, device_id=dev
        )

    def push(src, dst, send, recv, dev):
        copy = remote(src, dst, send, recv, dev)
        copy.start()
        pending.append(copy)

    def shard(z_hi, y, c):
        return (z_hi * NY + y) * 2 + c

    own_d = shard(zh, yy, core)
    oth = 1 - zh
    bufs = (we, w1, w2)

    loads = [
        pltpu.make_async_copy(wex_ref, we.at[own_d], lsem.at[0]),
        pltpu.make_async_copy(wpr_ref, w1.at[own_d], lsem.at[1]),
        pltpu.make_async_copy(f_ref, fbuf, lsem.at[2]),
        pltpu.make_async_copy(wqkv_ref, w2.at[own_d, 0:96], lsem.at[3]),
        pltpu.make_async_copy(wout_ref, w2.at[own_d, 96:128], lsem.at[4]),
    ]
    for load in loads:
        load.start()
    pl.semaphore_wait(barrier, len(peers))

    odd = xx % 2
    unit = (128, 512, 32)

    def piece(ph, d, first, count):
        span = pl.ds(pl.multiple_of(first * unit[ph], unit[ph]), count * unit[ph])
        return bufs[ph].at[d, :, span] if ph == 1 else bufs[ph].at[d, span]

    places = [
        (oth, yy), (zh, y_dn), (zh, y_up), (zh, y_far), (oth, y_dn), (oth, y_up), (oth, y_far), (zh, yy)
    ]

    def wpush(ph, slot, ref, dev):
        push(ref, ref, wsend.at[ph, slot], wrecv.at[ph, slot], dev)

    def wwait(ph, slot, ref):
        remote(ref, ref, wsend.at[ph, slot], wrecv.at[ph, slot], dev_sib).wait_recv()

    def carried(ph, i):
        return piece(ph, shard(*places[i], core), 2 * odd, 2)

    def spread(ph, i, base):
        ref = carried(ph, i)
        wpush(ph, base, ref, dev_up)
        wpush(ph, base + 1, ref, dev_dn)
        wpush(ph, base + 2, ref, dev_far)

    def g_start(ph):
        wpush(ph, 0, carried(ph, 7), dev_mir)
        spread(ph, 7, 1)
        wpush(ph, 21, bufs[ph].at[own_d], dev_sib)

    def g_arrive(ph, *which):
        for i in which:
            wwait(ph, i, carried(ph, i))
            if i == 0:
                spread(ph, 0, 4)
            d = shard(*places[i], core)
            wpush(ph, 7 + 2 * i, piece(ph, d, 2 * odd, 1), dev_xup)
            wpush(ph, 8 + 2 * i, piece(ph, d, 2 * odd + 1, 1), dev_xdn)

    def g_finish(ph, *which):
        for i in which:
            d = shard(*places[i], core)
            wwait(ph, 7 + 2 * i, piece(ph, d, 2 - 2 * odd, 1))
            wwait(ph, 8 + 2 * i, piece(ph, d, 3 - 2 * odd, 1))
            wpush(ph, 22 + i, bufs[ph].at[d], dev_sib)

    def sib_wait(ph, *which):
        for i in which:
            slot = 21 if i == 7 else 22 + i
            wwait(ph, slot, bufs[ph].at[shard(*places[i], 1 - core)])

    loads[0].wait()
    g_start(0)
    push(f_ref.at[ROWS - 1], halo.at[0], hsend.at[0], hrecv.at[0], dev_next)
    push(f_ref.at[0], halo.at[1], hsend.at[1], hrecv.at[1], dev_prev)
    loads[1].wait()
    g_start(1)

    tok = lax.broadcasted_iota(jnp.int32, (COLS, COLS), 0)
    col = lax.broadcasted_iota(jnp.int32, (COLS, COLS), 1)
    perm = ((tok % 8) * 16 + tok // 8 == col).astype(BF16)

    def prep(row, value):
        moved = dot_nn(perm, value)
        xn[row] = (moved * bns_ref[...] + bnb_ref[...]).astype(BF16)
        return moved.astype(BF16)

    loads[2].wait()

    @pl.loop(0, ROWS)
    def _(r):
        fperm[r] = prep(r + 1, fbuf[r])

    sub = lax.broadcasted_iota(jnp.int32, (2, 8, 128), 1)

    def expanded(x, g):
        w = jnp.concatenate([we[2 * g], we[2 * g + 1]], axis=1)
        bias = be_ref[:, pl.ds(pl.multiple_of(256 * g, 256), 256)]
        return gelu(dot_nn(x, w) + bias)

    def store(g, e, put):
        for k in range(2):
            part = e[:, 128 * k : 128 * (k + 1)].reshape(2, 16, 8, 128)
            before = jnp.where(sub == 0, 0.0, pltpu.roll(part[:, 15], 1, 1))
            after = jnp.where(sub == 7, 0.0, pltpu.roll(part[:, 0], 7, 1))
            put(2 * g + k, slice(1, 17), part)
            put(2 * g + k, 0, before)
            put(2 * g + k, 17, after)

    def expand(i):
        z_hi, y = places[i]
        g = z_hi * NY + y

        @pl.loop(0, ROWS // 2)
        def _(r2):
            rows = pl.ds(2 * r2 + 1, 2)

            def put(l, b, value):
                ebuf[l, rows, b] = value

            store(g, expanded(xn[rows].reshape(2 * COLS, CH), g), put)

    def expand_rim():
        remote(halo.at[0], halo.at[0], hsend.at[0], hrecv.at[0], dev_next).wait_recv()
        remote(halo.at[1], halo.at[1], hsend.at[1], hrecv.at[1], dev_prev).wait_recv()
        prep(0, halo[0])
        prep(ROWS + 1, halo[1])

        @pl.loop(0, 8)
        def _(g):
            x = jnp.concatenate([xn[0], xn[ROWS + 1]], axis=0)

            def put(l, b, value):
                ebuf[l, 0, b] = value[0]
                ebuf[l, ROWS + 1, b] = value[1]

            store(g, expanded(x, g), put)

        @pl.when(sp == 0)
        def _():
            ebuf[:, 0] = jnp.zeros((16, 18, 8, 128), F32)

        @pl.when(sp == 15)
        def _():
            ebuf[:, ROWS + 1] = jnp.zeros((16, 18, 8, 128), F32)

    sib_wait(0, 7)
    g_arrive(0, 1, 2, 3)
    expand(7)
    g_arrive(0, 0)
    g_finish(0, 1, 2, 3)
    sib_wait(0, 1)
    expand(1)
    g_arrive(1, 1, 2, 3)
    g_finish(0, 0)
    sib_wait(0, 2)
    expand(2)
    g_arrive(1, 0)
    sib_wait(0, 3)
    expand(3)
    g_arrive(0, 4, 5, 6)
    sib_wait(0, 0)
    expand(0)
    g_finish(0, 4, 5, 6)
    loads[3].wait()
    loads[4].wait()
    g_start(2)
    g_finish(1, 1, 2, 3, 0)
    sib_wait(0, 4)
    expand(4)
    g_arrive(1, 4, 5, 6)
    sib_wait(0, 5)
    expand(5)
    sib_wait(0, 6)
    expand(6)
    g_finish(1, 4, 5, 6)
    expand_rim()

    def conv(q):
        @pl.loop(0, 8)
        def _(g):
            for k in range(2):
                lanes = pl.ds(pl.multiple_of(256 * g + 128 * k, 128), 128)
                bias = dwb_ref[:, lanes]
                for r in range(2):
                    acc = jnp.broadcast_to(bias[None], (16, 8, 128))
                    for i in range(3):
                        for j in range(3):
                            tap = dwk_ref[i, j : j + 1, lanes]
                            acc = acc + ebuf[2 * g + k, 2 * q + r + i, j : j + 16] * tap[None]
                    sbuf[g, 128 * r : 128 * (r + 1), 128 * k : 128 * (k + 1)] = (
                        gelu(acc).astype(BF16).reshape(128, 128)
                    )

    def project(q):
        w = w1[...].reshape(CH, FF)
        total = fperm[2 * q : 2 * q + 2].reshape(2 * COLS, CH).astype(F32)
        for g in range(8):
            total = total + dot_nt(sbuf[g], w[:, 256 * g : 256 * (g + 1)])
        co[2 * q : 2 * q + 2] = total.astype(BF16).reshape(2, COLS, CH)

    def group(k):
        return pl.ds(pl.multiple_of(16 * k, 16), 16)

    def forward(q):
        rows = pl.ds(2 * q, 2)
        for m in range(1, 8):
            k = (mine + m) % 8
            push(
                co.at[rows, group(k)], gbuf.at[rows, mine], asend.at[q, m - 1], arecv.at[q, m - 1], member(k)
            )
        gbuf[rows, mine] = co[rows, group(mine)]

    def arrived(q):
        rows = pl.ds(2 * q, 2)
        for m in range(1, 8):
            k = (mine + 8 - m) % 8
            ref = gbuf.at[rows, k]
            remote(ref, ref, asend.at[q, m - 1], arecv.at[q, m - 1], member(k)).wait_recv()

    lane = lax.broadcasted_iota(jnp.int32, (128, 128), 1)
    row = lax.broadcasted_iota(jnp.int32, (128, 128), 0)
    heads = [(lane // 32 == n) for n in range(4)]
    same = (lane // 8) % 2 == (row // 8) % 2
    same4 = jnp.concatenate([same] * 4, axis=0)

    def attend(q):
        held = gbuf[2 * q : 2 * q + 2].reshape(256, CH).astype(F32)
        center = jnp.mean(held, axis=-1, keepdims=True)
        off = held - center
        spread_of = jnp.mean(off * off, axis=-1, keepdims=True)
        ln = (off * lax.rsqrt(spread_of + 1e-05) * lng_ref[...] + lnb_ref[...]).astype(BF16)
        w = w2[:, 0:96].reshape(3 * CH, CH)
        qkv[:, 0:CH] = (dot_nt(ln, w[0:CH]) * Q_SCALE).astype(BF16)
        qkv[:, CH : 2 * CH] = dot_nt(ln, w[CH : 2 * CH]).astype(BF16)
        qkv[:, 2 * CH :] = dot_nt(ln, w[2 * CH :]).astype(BF16)

        @pl.loop(0, 2)
        def _(r):
            rows = pl.ds(pl.multiple_of(128 * r, 128), 128)
            parts = []
            for gr in range(4):
                lo = 128 * gr
                qv = qkv[rows, lo : lo + 128]
                kv = qkv[rows, CH + lo : CH + lo + 128]
                vv = qkv[rows, 2 * CH + lo : 2 * CH + lo + 128]
                zero = jnp.zeros_like(qv)
                qm = jnp.concatenate([jnp.where(m, qv, zero) for m in heads], axis=0)
                vm = jnp.concatenate([jnp.where(m, vv, zero) for m in heads], axis=0)
                e = jnp.where(same4, jnp.exp2(dot_nt(qm, kv)), 0.0)
                p = (e * (1.0 / jnp.sum(e, axis=1, keepdims=True))).astype(BF16)
                wide = jnp.concatenate([p[128 * n : 128 * (n + 1)] for n in range(4)], axis=1)
                parts.append(dot_nn(wide, vm).astype(BF16))
            done = dot_nt(jnp.concatenate(parts, axis=1), w2[:, 96:128].reshape(CH, CH))
            done = done + gbuf[2 * q + r].reshape(128, CH).astype(F32)
            fin[2 * q + r] = done.astype(BF16).reshape(8, 16, CH)

    keeps = []

    def send_back(q):
        rows = pl.ds(2 * q, 2)
        for m in range(1, 8):
            k = (mine + m) % 8
            push(
                fin.at[rows, k], o_ref.at[rows, group(mine)], rsend.at[q, m - 1], rrecv.at[q, m - 1], member(k)
            )
        keep = pltpu.make_async_copy(fin.at[rows, mine], o_ref.at[rows, group(mine)], lsem.at[5 + q])
        keep.start()
        keeps.append(keep)

    def returned(q):
        rows = pl.ds(2 * q, 2)
        for m in range(1, 8):
            k = (mine + 8 - m) % 8
            ref = o_ref.at[rows, group(k)]
            remote(ref, ref, rsend.at[q, m - 1], rrecv.at[q, m - 1], member(k)).wait_recv()

    conv(0)
    sib_wait(1, *range(8))
    project(0)
    forward(0)
    g_arrive(2, 1, 2, 3, 0)
    conv(1)
    project(1)
    forward(1)
    g_arrive(2, 4, 5, 6)
    g_finish(2, 1, 2, 3, 0)
    conv(2)
    project(2)
    forward(2)
    g_finish(2, 4, 5, 6)
    sib_wait(2, *range(8))
    arrived(0)
    attend(0)
    send_back(0)
    conv(3)
    project(3)
    forward(3)
    for q in range(1, 4):
        arrived(q)
        attend(q)
        send_back(q)
    for q in range(4):
        keeps[q].wait()
        returned(q)
    for copy in pending:
        copy.wait_send()


def local(
    fields, bn_scale, bn_shift, w_expand, expand_bias, dw_kernel, dw_bias, w_project, ln_gain, ln_bias, w_qkv, w_out
):
    vmem = pl.BlockSpec(memory_space=pltpu.VMEM)
    hbm = pl.BlockSpec(memory_space=pl.ANY)
    dma = pltpu.SemaphoreType.DMA
    out = pl.pallas_call(
        kernel,
        out_shape=jax.ShapeDtypeStruct((ROWS, COLS, CH), BF16),
        in_specs=[hbm, vmem, vmem, hbm, vmem, vmem, vmem, hbm, vmem, vmem, hbm, hbm],
        out_specs=hbm,
        scratch_shapes=[
            pltpu.VMEM((ROWS, COLS, CH), BF16),
            pltpu.VMEM((2, COLS, CH), BF16),
            pltpu.VMEM((ROWS, COLS, CH), BF16),
            pltpu.VMEM((ROWS + 2, COLS, CH), BF16),
            pltpu.VMEM((16, CH, 128), BF16),
            pltpu.VMEM((16, 32, FF), BF16),
            pltpu.VMEM((16, 128, CH), BF16),
            pltpu.VMEM((16, ROWS + 2, 18, 8, 128), F32),
            pltpu.VMEM((8, 256, 256), BF16),
            pltpu.VMEM((ROWS, COLS, CH), BF16),
            pltpu.VMEM((ROWS, 8, 16, CH), BF16),
            pltpu.VMEM((256, 3 * CH), BF16),
            pltpu.VMEM((ROWS, 8, 16, CH), BF16),
            dma((9,)),
            dma((3, 29)),
            dma((3, 29)),
            dma((2,)),
            dma((2,)),
            dma((4, 7)),
            dma((4, 7)),
            dma((4, 7)),
            dma((4, 7)),
        ],
        compiler_params=pltpu.CompilerParams(
            collective_id=0, has_side_effects=True, vmem_limit_bytes=60 * 1024 * 1024
        ),
    )(
        fields.reshape(ROWS, COLS, CH),
        bn_scale.reshape(1, CH),
        bn_shift.reshape(1, CH),
        w_expand,
        expand_bias.reshape(1, FF),
        dw_kernel,
        dw_bias.reshape(1, FF),
        w_project.T,
        ln_gain.reshape(1, CH),
        ln_bias.reshape(1, CH),
        w_qkv.T,
        w_out.T,
    )
    return out.reshape(ROWS, 16, 8, CH).transpose(0, 2, 1, 3).reshape(fields.shape)


def solution(mesh):
    in_specs = (
        P("dp", "space", None, None),
        P(),
        P(),
        P(None, "dp"),
        P(),
        P(),
        P(),
        P(None, "dp"),
        P(),
        P(),
        P(None, "dp"),
        P(None, "dp"),
    )
    out_specs = P("dp", "space", None, None)
    return jax.shard_map(local, mesh=mesh, in_specs=in_specs, out_specs=out_specs, check_vma=False)
```

```python
import jax
import jax.numpy as jnp
from jax import lax
from jax.experimental import pallas as pl
from jax.experimental.pallas import tpu as pltpu
from jax.sharding import PartitionSpec as P

F32 = jnp.float32
BF16 = jnp.bfloat16
NY, NX, NZ = 4, 4, 4
ROWS, COLS, CH, FF = 8, 128, 512, 2048
Q_SCALE = 1.4426950408889634 / (32.0**0.5)


def dot_nn(a, b):
    return jnp.dot(a, b, preferred_element_type=F32)


def dot_nt(a, b):
    return lax.dot_general(a, b, (((1,), (1,)), ((), ())), preferred_element_type=F32)


def gelu(x):
    inner = x * (0.7978845608028654 + 0.035677408136300125 * (x * x))
    half = 0.5 * x
    return half + half * jnp.tanh(inner)


def kernel(
    f_ref, bns_ref, bnb_ref, wex_ref, be_ref, dwk_ref, dwb_ref, wpr_ref, lng_ref, lnb_ref, wqkv_ref, wout_ref,
    o_ref,
    fbuf, halo, fperm, xn, we, w1, w2, ebuf, sbuf, co, gbuf, qkv, fin,
    lsem, wsend, wrecv, fsend, frecv, hsend, hrecv, asend, arecv, rsend, rrecv,
):
    dp = lax.axis_index("dp")
    sp = lax.axis_index("space")
    core, yy, zh = dp % 2, (dp // 2) % NY, dp // (2 * NY)
    xx, zl = sp // NZ, sp % NZ
    par, mine = zl // 2, 2 * xx + zl % 2
    band = 2 * mine + par
    home = sp // 2
    traded = (zl == 1) | (zl == 2)

    def at(z_hi, y, c, x, z_lo):
        return {"dp": (z_hi * NY + y) * 2 + c, "space": x * NZ + z_lo}

    y_up, y_dn, y_far = (yy + 1) % NY, (yy + NY - 1) % NY, (yy + 2) % NY
    dev_up = at(zh, y_up, core, xx, zl)
    dev_dn = at(zh, y_dn, core, xx, zl)
    dev_far = at(zh, y_far, core, xx, zl)
    dev_sib = at(zh, yy, 1 - core, xx, zl)
    dev_mir = at(1 - zh, yy, core, xx, NZ - 1 - zl)
    dev_xup = at(zh, yy, core, (xx + 1) % NX, zl)
    dev_xdn = at(zh, yy, core, (xx + NX - 1) % NX, zl)
    dev_trade = at(zh, yy, core, xx, NZ - 1 - zl)
    last_x, last_z = (xx + zl // 3) % NX, jnp.where(zl == 0, 2, jnp.where(zl == 2, 3, 0))
    first_x, first_z = jnp.where(zl == 0, xx + NX - 1, xx) % NX, jnp.where(zl == 0, 3, jnp.where(zl == 3, 1, 0))
    dev_last = at(zh, yy, core, last_x, last_z)
    dev_first = at(zh, yy, core, first_x, first_z)

    def member(k):
        return {"dp": dp, "space": (k // 2) * NZ + 2 * par + k % 2}

    def owner(k):
        return {"dp": dp, "space": 2 * k + par}

    barrier = pltpu.get_barrier_semaphore()
    peers = [dev_up, dev_dn, dev_far, dev_sib, dev_mir]
    peers += [{"dp": dp, "space": (sp + m) % 16} for m in range(1, 16)]
    for peer in peers:
        pl.semaphore_signal(barrier, inc=1, device_id=peer)

    pending = []

    def remote(src, dst, send, recv, dev):
        return pltpu.make_async_remote_copy(
            src_ref=src, dst_ref=dst, send_sem=send, recv_sem=recv, device_id=dev
        )

    def push(src, dst, send, recv, dev):
        copy = remote(src, dst, send, recv, dev)
        copy.start()
        pending.append(copy)

    guarded = []

    def push_if(cond, src, dst, send, recv, dev):
        copy = remote(src, dst, send, recv, dev)
        pl.when(cond)(copy.start)
        guarded.append((cond, copy))

    def shard(z_hi, y, c):
        return (z_hi * NY + y) * 2 + c

    own_d = shard(zh, yy, core)
    oth = 1 - zh
    bufs = (we, w1, w2)

    loads = [
        pltpu.make_async_copy(wex_ref, we.at[own_d], lsem.at[0]),
        pltpu.make_async_copy(wpr_ref, w1.at[own_d], lsem.at[1]),
        pltpu.make_async_copy(wqkv_ref, w2.at[own_d, 0:96], lsem.at[2]),
        pltpu.make_async_copy(wout_ref, w2.at[own_d, 96:128], lsem.at[3]),
    ]
    for load in loads:
        load.start()

    def pair(q):
        return pl.ds(2 * q, 2)

    stays = [(jnp.logical_not(traded), f_ref.at[pair(q)], fbuf.at[pair(q)], frecv.at[q]) for q in range(4)]
    stays += [(zl == 1, f_ref.at[ROWS - 1], halo.at[0], hrecv.at[0]), (zl == 2, f_ref.at[0], halo.at[1], hrecv.at[1])]
    for cond, src, dst, sem in stays:
        pl.when(cond)(pltpu.make_async_copy(src, dst, sem).start)
    pl.semaphore_wait(barrier, len(peers))

    odd = xx % 2
    unit = (128, 512, 32)

    def piece(ph, d, first, count):
        span = pl.ds(pl.multiple_of(first * unit[ph], unit[ph]), count * unit[ph])
        return bufs[ph].at[d, :, span] if ph == 1 else bufs[ph].at[d, span]

    places = [
        (oth, yy), (zh, y_dn), (zh, y_up), (zh, y_far), (oth, y_dn), (oth, y_up), (oth, y_far), (zh, yy)
    ]

    def wpush(ph, slot, ref, dev):
        push(ref, ref, wsend.at[ph, slot], wrecv.at[ph, slot], dev)

    def wwait(ph, slot, ref):
        remote(ref, ref, wsend.at[ph, slot], wrecv.at[ph, slot], dev_sib).wait_recv()

    def carried(ph, i):
        return piece(ph, shard(*places[i], core), 2 * odd, 2)

    def spread(ph, i, base):
        ref = carried(ph, i)
        wpush(ph, base, ref, dev_up)
        wpush(ph, base + 1, ref, dev_dn)
        wpush(ph, base + 2, ref, dev_far)

    def g_start(ph):
        wpush(ph, 0, carried(ph, 7), dev_mir)
        spread(ph, 7, 1)
        wpush(ph, 21, bufs[ph].at[own_d], dev_sib)

    def g_arrive(ph, *which):
        for i in which:
            wwait(ph, i, carried(ph, i))
            if i == 0:
                spread(ph, 0, 4)
            d = shard(*places[i], core)
            wpush(ph, 7 + 2 * i, piece(ph, d, 2 * odd, 1), dev_xup)
            wpush(ph, 8 + 2 * i, piece(ph, d, 2 * odd + 1, 1), dev_xdn)

    def g_finish(ph, *which):
        for i in which:
            d = shard(*places[i], core)
            wwait(ph, 7 + 2 * i, piece(ph, d, 2 - 2 * odd, 1))
            wwait(ph, 8 + 2 * i, piece(ph, d, 3 - 2 * odd, 1))
            wpush(ph, 22 + i, bufs[ph].at[d], dev_sib)

    def sib_wait(ph, *which):
        for i in which:
            slot = 21 if i == 7 else 22 + i
            wwait(ph, slot, bufs[ph].at[shard(*places[i], 1 - core)])

    loads[0].wait()
    g_start(0)
    push_if(zl != 1, f_ref.at[ROWS - 1], halo.at[0], hsend.at[0], hrecv.at[0], dev_last)
    for q in range(4):
        push_if(traded, f_ref.at[pair(q)], fbuf.at[pair(q)], fsend.at[q], frecv.at[q], dev_trade)
    push_if(zl != 2, f_ref.at[0], halo.at[1], hsend.at[1], hrecv.at[1], dev_first)
    loads[1].wait()
    g_start(1)

    tok = lax.broadcasted_iota(jnp.int32, (COLS, COLS), 0)
    col = lax.broadcasted_iota(jnp.int32, (COLS, COLS), 1)
    perm = ((tok % 8) * 16 + tok // 8 == col).astype(BF16)

    def prep(row, value):
        moved = dot_nn(perm, value)
        xn[row] = (moved * bns_ref[...] + bnb_ref[...]).astype(BF16)
        return moved.astype(BF16)

    def take(q):
        remote(fbuf.at[pair(q)], fbuf.at[pair(q)], fsend.at[q], frecv.at[q], dev_trade).wait_recv()
        for r in range(2 * q, 2 * q + 2):
            fperm[r] = prep(r + 1, fbuf[r])

    def expand_rows(first, count, g):
        w = jnp.concatenate([we[2 * g], we[2 * g + 1]], axis=1)
        bias = be_ref[:, pl.ds(pl.multiple_of(256 * g, 256), 256)]
        rows = slice(first, first + count)
        e = gelu(dot_nn(xn[rows].reshape(count * COLS, CH), w) + bias)
        sub = lax.broadcasted_iota(jnp.int32, (count, 8, 128), 1)
        for k in range(2):
            part = e[:, 128 * k : 128 * (k + 1)].reshape(count, 16, 8, 128)
            ebuf[2 * g + k, rows, 1:17] = part
            ebuf[2 * g + k, rows, 0] = jnp.where(sub == 0, 0.0, pltpu.roll(part[:, 15], 1, 1))
            ebuf[2 * g + k, rows, 17] = jnp.where(sub == 7, 0.0, pltpu.roll(part[:, 0], 7, 1))

    def early(i):
        sib_wait(0, i)
        z_hi, y = places[i]
        expand_rows(1, 2, z_hi * NY + y)

    def expand(q):
        take(q)

        @pl.loop(0, 8)
        def _(g):
            expand_rows(2 * q + 1, 2, g)

    def expand_rim(side):
        remote(halo.at[side], halo.at[side], hsend.at[side], hrecv.at[side], dev_trade).wait_recv()
        at_row = (ROWS + 1) * side
        prep(at_row, halo[side])

        @pl.loop(0, 8)
        def _(g):
            expand_rows(at_row, 1, g)

        @pl.when(band == 15 * side)
        def _():
            ebuf[:, at_row] = jnp.zeros((16, 18, 8, 128), F32)

    g_arrive(0, 1, 2, 3, 0)
    g_arrive(1, 1, 2, 3, 0)
    take(0)
    early(7)
    g_finish(0, 1, 2, 3)
    early(1)
    g_finish(0, 0)
    early(2)
    g_arrive(0, 4, 5, 6)
    early(3)
    g_finish(1, 1, 2, 3)
    early(0)
    g_finish(0, 4, 5, 6)
    g_arrive(1, 4, 5, 6)
    early(4)
    g_finish(1, 0)
    early(5)
    early(6)
    loads[2].wait()
    loads[3].wait()
    g_start(2)
    expand(1)
    g_finish(1, 4, 5, 6)
    expand_rim(0)

    def conv(q):
        @pl.loop(0, 8)
        def _(g):
            for k in range(2):
                lanes = pl.ds(pl.multiple_of(256 * g + 128 * k, 128), 128)
                bias = dwb_ref[:, lanes]
                for r in range(2):
                    acc = jnp.broadcast_to(bias[None], (16, 8, 128))
                    for i in range(3):
                        for j in range(3):
                            tap = dwk_ref[i, j : j + 1, lanes]
                            acc = acc + ebuf[2 * g + k, 2 * q + r + i, j : j + 16] * tap[None]
                    sbuf[g, 128 * r : 128 * (r + 1), 128 * k : 128 * (k + 1)] = (
                        gelu(acc).astype(BF16).reshape(128, 128)
                    )

    def project(q):
        w = w1[...].reshape(CH, FF)
        total = fperm[2 * q : 2 * q + 2].reshape(2 * COLS, CH).astype(F32)
        for g in range(8):
            total = total + dot_nt(sbuf[g], w[:, 256 * g : 256 * (g + 1)])
        co[2 * q : 2 * q + 2] = total.astype(BF16).reshape(2, COLS, CH)

    def group(k):
        return pl.ds(pl.multiple_of(16 * k, 16), 16)

    def forward(q):
        rows = pl.ds(2 * q, 2)
        for m in range(1, 8):
            k = (mine + m) % 8
            push(
                co.at[rows, group(k)], gbuf.at[rows, mine], asend.at[q, m - 1], arecv.at[q, m - 1], member(k)
            )
        gbuf[rows, mine] = co[rows, group(mine)]

    def arrived(q):
        rows = pl.ds(2 * q, 2)
        for m in range(1, 8):
            k = (mine + 8 - m) % 8
            ref = gbuf.at[rows, k]
            remote(ref, ref, asend.at[q, m - 1], arecv.at[q, m - 1], member(k)).wait_recv()

    lane = lax.broadcasted_iota(jnp.int32, (128, 128), 1)
    row = lax.broadcasted_iota(jnp.int32, (128, 128), 0)
    heads = [(lane // 32 == n) for n in range(4)]
    same = (lane // 8) % 2 == (row // 8) % 2
    same4 = jnp.concatenate([same] * 4, axis=0)

    def attend(q):
        held = gbuf[2 * q : 2 * q + 2].reshape(256, CH).astype(F32)
        center = jnp.mean(held, axis=-1, keepdims=True)
        off = held - center
        spread_of = jnp.mean(off * off, axis=-1, keepdims=True)
        ln = (off * lax.rsqrt(spread_of + 1e-05) * lng_ref[...] + lnb_ref[...]).astype(BF16)
        w = w2[:, 0:96].reshape(3 * CH, CH)
        qkv[:, 0:CH] = (dot_nt(ln, w[0:CH]) * Q_SCALE).astype(BF16)
        qkv[:, CH : 2 * CH] = dot_nt(ln, w[CH : 2 * CH]).astype(BF16)
        qkv[:, 2 * CH :] = dot_nt(ln, w[2 * CH :]).astype(BF16)

        @pl.loop(0, 2)
        def _(r):
            rows = pl.ds(pl.multiple_of(128 * r, 128), 128)
            parts = []
            for gr in range(4):
                lo = 128 * gr
                qv = qkv[rows, lo : lo + 128]
                kv = qkv[rows, CH + lo : CH + lo + 128]
                vv = qkv[rows, 2 * CH + lo : 2 * CH + lo + 128]
                zero = jnp.zeros_like(qv)
                qm = jnp.concatenate([jnp.where(m, qv, zero) for m in heads], axis=0)
                vm = jnp.concatenate([jnp.where(m, vv, zero) for m in heads], axis=0)
                e = jnp.where(same4, jnp.exp2(dot_nt(qm, kv)), 0.0)
                p = (e * (1.0 / jnp.sum(e, axis=1, keepdims=True))).astype(BF16)
                wide = jnp.concatenate([p[128 * n : 128 * (n + 1)] for n in range(4)], axis=1)
                parts.append(dot_nn(wide, vm).astype(BF16))
            done = dot_nt(jnp.concatenate(parts, axis=1), w2[:, 96:128].reshape(CH, CH))
            done = done + gbuf[2 * q + r].reshape(128, CH).astype(F32)
            fin[2 * q + r] = done.astype(BF16).reshape(8, 16, CH)

    def send_back(q):
        rows = pl.ds(2 * q, 2)
        for m in range(8):
            k = (mine + m) % 8
            src, dst = fin.at[rows, k], o_ref.at[rows, group(mine)]
            if m == 0:
                push_if(traded, src, dst, rsend.at[q, m], rrecv.at[q, m], owner(k))
                keep = pltpu.make_async_copy(src, dst, rrecv.at[q, m])
                pl.when(jnp.logical_not(traded))(keep.start)
            else:
                push(src, dst, rsend.at[q, m], rrecv.at[q, m], owner(k))

    def returned(q):
        rows = pl.ds(2 * q, 2)
        for m in range(8):
            ref = o_ref.at[rows, group((home + 8 - m) % 8)]
            remote(ref, ref, rsend.at[q, m], rrecv.at[q, m], dev_trade).wait_recv()

    conv(0)
    sib_wait(1, *range(8))
    project(0)
    forward(0)
    g_arrive(2, 1, 2, 3, 0)
    expand(2)
    conv(1)
    project(1)
    forward(1)
    g_arrive(2, 4, 5, 6)
    g_finish(2, 1, 2, 3, 0)
    expand(3)
    g_finish(2, 4, 5, 6)
    sib_wait(2, *range(8))
    arrived(0)
    attend(0)
    send_back(0)
    expand_rim(1)
    conv(2)
    project(2)
    forward(2)
    arrived(1)
    attend(1)
    send_back(1)
    conv(3)
    project(3)
    forward(3)
    for q in range(2, 4):
        arrived(q)
        attend(q)
        send_back(q)
    for q in range(4):
        returned(q)
    for copy in pending:
        copy.wait_send()
    for cond, copy in guarded:
        pl.when(cond)(copy.wait_send)


def local(
    fields, bn_scale, bn_shift, w_expand, expand_bias, dw_kernel, dw_bias, w_project, ln_gain, ln_bias, w_qkv, w_out
):
    vmem = pl.BlockSpec(memory_space=pltpu.VMEM)
    hbm = pl.BlockSpec(memory_space=pl.ANY)
    dma = pltpu.SemaphoreType.DMA
    out = pl.pallas_call(
        kernel,
        out_shape=jax.ShapeDtypeStruct((ROWS, COLS, CH), BF16),
        in_specs=[hbm, vmem, vmem, hbm, vmem, vmem, vmem, hbm, vmem, vmem, hbm, hbm],
        out_specs=hbm,
        scratch_shapes=[
            pltpu.VMEM((ROWS, COLS, CH), BF16),
            pltpu.VMEM((2, COLS, CH), BF16),
            pltpu.VMEM((ROWS, COLS, CH), BF16),
            pltpu.VMEM((ROWS + 2, COLS, CH), BF16),
            pltpu.VMEM((16, CH, 128), BF16),
            pltpu.VMEM((16, 32, FF), BF16),
            pltpu.VMEM((16, 128, CH), BF16),
            pltpu.VMEM((16, ROWS + 2, 18, 8, 128), F32),
            pltpu.VMEM((8, 256, 256), BF16),
            pltpu.VMEM((ROWS, COLS, CH), BF16),
            pltpu.VMEM((ROWS, 8, 16, CH), BF16),
            pltpu.VMEM((256, 3 * CH), BF16),
            pltpu.VMEM((ROWS, 8, 16, CH), BF16),
            dma((4,)),
            dma((3, 29)),
            dma((3, 29)),
            dma((4,)),
            dma((4,)),
            dma((2,)),
            dma((2,)),
            dma((4, 7)),
            dma((4, 7)),
            dma((4, 8)),
            dma((4, 8)),
        ],
        compiler_params=pltpu.CompilerParams(
            collective_id=0, has_side_effects=True, vmem_limit_bytes=60 * 1024 * 1024
        ),
    )(
        fields.reshape(ROWS, COLS, CH),
        bn_scale.reshape(1, CH),
        bn_shift.reshape(1, CH),
        w_expand,
        expand_bias.reshape(1, FF),
        dw_kernel,
        dw_bias.reshape(1, FF),
        w_project.T,
        ln_gain.reshape(1, CH),
        ln_bias.reshape(1, CH),
        w_qkv.T,
        w_out.T,
    )
    return out.reshape(ROWS, 16, 8, CH).transpose(0, 2, 1, 3).reshape(fields.shape)


def solution(mesh):
    in_specs = (
        P("dp", "space", None, None),
        P(),
        P(),
        P(None, "dp"),
        P(),
        P(),
        P(),
        P(None, "dp"),
        P(),
        P(),
        P(None, "dp"),
        P(None, "dp"),
    )
    out_specs = P("dp", "space", None, None)
    return jax.shard_map(local, mesh=mesh, in_specs=in_specs, out_specs=out_specs, check_vma=False)
```

```python
import jax
import jax.numpy as jnp
from jax import lax
from jax.experimental import pallas as pl
from jax.experimental.pallas import tpu as pltpu
from jax.sharding import PartitionSpec as P

F32 = jnp.float32
BF16 = jnp.bfloat16
NY, NX, NZ = 4, 4, 4
ROWS, COLS, CH, FF = 8, 128, 512, 2048
Q_SCALE = 1.4426950408889634 / (32.0**0.5)


def dot_nn(a, b):
    return jnp.dot(a, b, preferred_element_type=F32)


def dot_nt(a, b):
    return lax.dot_general(a, b, (((1,), (1,)), ((), ())), preferred_element_type=F32)


def gelu(x):
    inner = x * (0.7978845608028654 + 0.035677408136300125 * (x * x))
    half = 0.5 * x
    return half + half * jnp.tanh(inner)


def kernel(
    f_ref, bns_in, bnb_in, wex_ref, be_in, dwk_in, dwb_in, wpr_ref, lng_in, lnb_in, wqkv_ref, wout_ref,
    o_ref,
    bns_ref, bnb_ref, be_ref, dwk_ref, dwb_ref, lng_ref, lnb_ref,
    fbuf, halo, fperm, xn, we, w1, w2, ebuf, sbuf, co, gbuf, qkv, fin,
    lsem, wsend, wrecv, fsend, frecv, hsend, hrecv, asend, arecv, rsend, rrecv,
):
    dp = lax.axis_index("dp")
    sp = lax.axis_index("space")
    core, yy, zh = dp % 2, (dp // 2) % NY, dp // (2 * NY)
    xx, zl = sp // NZ, sp % NZ
    par, mine = zl // 2, 2 * xx + zl % 2
    band = 2 * mine + par
    home = sp // 2
    traded = (zl == 1) | (zl == 2)

    def at(z_hi, y, c, x, z_lo):
        return {"dp": (z_hi * NY + y) * 2 + c, "space": x * NZ + z_lo}

    y_up, y_dn, y_far = (yy + 1) % NY, (yy + NY - 1) % NY, (yy + 2) % NY
    dev_up = at(zh, y_up, core, xx, zl)
    dev_dn = at(zh, y_dn, core, xx, zl)
    dev_far = at(zh, y_far, core, xx, zl)
    dev_sib = at(zh, yy, 1 - core, xx, zl)
    dev_mir = at(1 - zh, yy, core, xx, NZ - 1 - zl)
    dev_xup = at(zh, yy, core, (xx + 1) % NX, zl)
    dev_xdn = at(zh, yy, core, (xx + NX - 1) % NX, zl)
    dev_trade = at(zh, yy, core, xx, NZ - 1 - zl)
    last_x, last_z = (xx + zl // 3) % NX, jnp.where(zl == 0, 2, jnp.where(zl == 2, 3, 0))
    first_x, first_z = jnp.where(zl == 0, xx + NX - 1, xx) % NX, jnp.where(zl == 0, 3, jnp.where(zl == 3, 1, 0))
    dev_last = at(zh, yy, core, last_x, last_z)
    dev_first = at(zh, yy, core, first_x, first_z)

    def member(k):
        return {"dp": dp, "space": (k // 2) * NZ + 2 * par + k % 2}

    def owner(k):
        return {"dp": dp, "space": 2 * k + par}

    barrier = pltpu.get_barrier_semaphore()
    peers = [dev_up, dev_dn, dev_far, dev_sib, dev_mir]
    peers += [{"dp": dp, "space": (sp + m) % 16} for m in range(1, 16)]
    for peer in peers:
        pl.semaphore_signal(barrier, inc=1, device_id=peer)

    pending = []

    def remote(src, dst, send, recv, dev):
        return pltpu.make_async_remote_copy(
            src_ref=src, dst_ref=dst, send_sem=send, recv_sem=recv, device_id=dev
        )

    def push(src, dst, send, recv, dev):
        copy = remote(src, dst, send, recv, dev)
        copy.start()
        pending.append(copy)

    guarded = []

    def push_if(cond, src, dst, send, recv, dev):
        copy = remote(src, dst, send, recv, dev)
        pl.when(cond)(copy.start)
        guarded.append((cond, copy))

    def shard(z_hi, y, c):
        return (z_hi * NY + y) * 2 + c

    own_d = shard(zh, yy, core)
    oth = 1 - zh
    bufs = (we, w1, w2)

    loads = [
        pltpu.make_async_copy(wex_ref, we.at[own_d], lsem.at[0]),
        pltpu.make_async_copy(wpr_ref, w1.at[own_d], lsem.at[1]),
        pltpu.make_async_copy(wqkv_ref, w2.at[own_d, 0:96], lsem.at[2]),
        pltpu.make_async_copy(wout_ref, w2.at[own_d, 96:128], lsem.at[3]),
    ]
    small = [
        (bns_in, bns_ref), (bnb_in, bnb_ref), (be_in, be_ref), (dwk_in, dwk_ref),
        (dwb_in, dwb_ref), (lng_in, lng_ref), (lnb_in, lnb_ref),
    ]
    loads += [pltpu.make_async_copy(src, dst, lsem.at[4 + n]) for n, (src, dst) in enumerate(small)]
    for load in loads:
        load.start()

    def pair(q):
        return pl.ds(2 * q, 2)

    stays = [(jnp.logical_not(traded), f_ref.at[pair(q)], fbuf.at[pair(q)], frecv.at[q]) for q in range(4)]
    stays += [(zl == 1, f_ref.at[ROWS - 1], halo.at[0], hrecv.at[0]), (zl == 2, f_ref.at[0], halo.at[1], hrecv.at[1])]
    for cond, src, dst, sem in stays:
        pl.when(cond)(pltpu.make_async_copy(src, dst, sem).start)
    pl.semaphore_wait(barrier, len(peers))

    odd = xx % 2
    unit = (128, 512, 32)

    def piece(ph, d, first, count):
        span = pl.ds(pl.multiple_of(first * unit[ph], unit[ph]), count * unit[ph])
        return bufs[ph].at[d, :, span] if ph == 1 else bufs[ph].at[d, span]

    places = [
        (oth, yy), (zh, y_dn), (zh, y_up), (zh, y_far), (oth, y_dn), (oth, y_up), (oth, y_far), (zh, yy)
    ]

    def wpush(ph, slot, ref, dev):
        push(ref, ref, wsend.at[ph, slot], wrecv.at[ph, slot], dev)

    def wwait(ph, slot, ref):
        remote(ref, ref, wsend.at[ph, slot], wrecv.at[ph, slot], dev_sib).wait_recv()

    def carried(ph, i):
        return piece(ph, shard(*places[i], core), 2 * odd, 2)

    def spread(ph, i, base):
        ref = carried(ph, i)
        wpush(ph, base, ref, dev_up)
        wpush(ph, base + 1, ref, dev_dn)
        wpush(ph, base + 2, ref, dev_far)

    def g_start(ph):
        wpush(ph, 0, carried(ph, 7), dev_mir)
        spread(ph, 7, 1)
        wpush(ph, 21, bufs[ph].at[own_d], dev_sib)

    def g_arrive(ph, *which):
        for i in which:
            wwait(ph, i, carried(ph, i))
            if i == 0:
                spread(ph, 0, 4)
            d = shard(*places[i], core)
            wpush(ph, 7 + 2 * i, piece(ph, d, 2 * odd, 1), dev_xup)
            wpush(ph, 8 + 2 * i, piece(ph, d, 2 * odd + 1, 1), dev_xdn)

    def g_finish(ph, *which):
        for i in which:
            d = shard(*places[i], core)
            wwait(ph, 7 + 2 * i, piece(ph, d, 2 - 2 * odd, 1))
            wwait(ph, 8 + 2 * i, piece(ph, d, 3 - 2 * odd, 1))
            wpush(ph, 22 + i, bufs[ph].at[d], dev_sib)

    def sib_wait(ph, *which):
        for i in which:
            slot = 21 if i == 7 else 22 + i
            wwait(ph, slot, bufs[ph].at[shard(*places[i], 1 - core)])

    loads[0].wait()
    g_start(0)
    push_if(zl != 1, f_ref.at[ROWS - 1], halo.at[0], hsend.at[0], hrecv.at[0], dev_last)
    for q in range(4):
        push_if(traded, f_ref.at[pair(q)], fbuf.at[pair(q)], fsend.at[q], frecv.at[q], dev_trade)
    push_if(zl != 2, f_ref.at[0], halo.at[1], hsend.at[1], hrecv.at[1], dev_first)
    loads[1].wait()
    g_start(1)

    tok = lax.broadcasted_iota(jnp.int32, (COLS, COLS), 0)
    col = lax.broadcasted_iota(jnp.int32, (COLS, COLS), 1)
    perm = ((tok % 8) * 16 + tok // 8 == col).astype(BF16)

    def prep(row, value):
        moved = dot_nn(perm, value)
        xn[row] = (moved * bns_ref[...] + bnb_ref[...]).astype(BF16)
        return moved.astype(BF16)

    def take(q):
        remote(fbuf.at[pair(q)], fbuf.at[pair(q)], fsend.at[q], frecv.at[q], dev_trade).wait_recv()
        for r in range(2 * q, 2 * q + 2):
            fperm[r] = prep(r + 1, fbuf[r])

    def expand_rows(first, count, *gs):
        rows = pl.ds(first, count)
        x = xn[rows].reshape(count * COLS, CH)
        sums = [dot_nn(x, jnp.concatenate([we[2 * g], we[2 * g + 1]], axis=1)) for g in gs]
        sub = lax.broadcasted_iota(jnp.int32, (count, 8, 128), 1)
        for g, summed in zip(gs, sums):
            e = gelu(summed + be_ref[:, pl.ds(pl.multiple_of(256 * g, 256), 256)])
            for k in range(2):
                part = e[:, 128 * k : 128 * (k + 1)].reshape(count, 16, 8, 128)
                ebuf[2 * g + k, rows, 1:17] = part
                ebuf[2 * g + k, rows, 0] = jnp.where(sub == 0, 0.0, pltpu.roll(part[:, 15], 1, 1))
                ebuf[2 * g + k, rows, 17] = jnp.where(sub == 7, 0.0, pltpu.roll(part[:, 0], 7, 1))

    def early(*which):
        sib_wait(0, *which)
        for i in which:
            z_hi, y = places[i]

            @pl.loop(0, 2)
            def _(q):
                expand_rows(2 * q + 1, 2, z_hi * NY + y)

    def expand(q):
        take(q)

        @pl.loop(0, 4)
        def _(g):
            expand_rows(2 * q + 1, 2, 2 * g, 2 * g + 1)

    def expand_rim(side):
        remote(halo.at[side], halo.at[side], hsend.at[side], hrecv.at[side], dev_trade).wait_recv()
        at_row = (ROWS + 1) * side
        prep(at_row, halo[side])

        @pl.loop(0, 4)
        def _(g):
            expand_rows(at_row, 1, 2 * g, 2 * g + 1)

        @pl.when(band == 15 * side)
        def _():
            ebuf[:, at_row] = jnp.zeros((16, 18, 8, 128), F32)

    g_arrive(0, 1, 2, 3, 0)
    g_arrive(1, 1, 2, 3, 0)
    loads[2].wait()
    loads[3].wait()
    g_start(2)
    for load in loads[4:]:
        load.wait()
    take(0)
    g_finish(0, 1, 2, 3, 0)
    g_arrive(0, 4, 5, 6)
    take(1)
    g_finish(1, 1, 2, 3, 0)
    early(7, 1)
    g_finish(0, 4, 5, 6)
    g_arrive(1, 4, 5, 6)
    early(2, 3, 0)
    g_finish(1, 4, 5, 6)
    early(4, 5, 6)
    g_arrive(2, 1, 2, 3, 0)
    expand_rim(0)

    def conv(q, g):
        for k in range(2):
            lanes = pl.ds(pl.multiple_of(256 * g + 128 * k, 128), 128)
            bias = dwb_ref[:, lanes]
            for r in range(2):
                summed = jnp.broadcast_to(bias[None], (16, 8, 128))
                for i in range(3):
                    for j in range(3):
                        tap = dwk_ref[i, j : j + 1, lanes]
                        summed = summed + ebuf[2 * g + k, 2 * q + r + i, j : j + 16] * tap[None]
                sbuf[g, 128 * r : 128 * (r + 1), 128 * k : 128 * (k + 1)] = (
                    gelu(summed).astype(BF16).reshape(128, 128)
                )

    def project(q):
        w = w1[...].reshape(CH, FF)
        total = fperm[2 * q : 2 * q + 2].reshape(2 * COLS, CH).astype(F32)
        for g in range(8):
            total = total + dot_nt(sbuf[g], w[:, 256 * g : 256 * (g + 1)])
        co[2 * q : 2 * q + 2] = total.astype(BF16).reshape(2, COLS, CH)

    def mbconv(q):
        @pl.loop(0, 8)
        def _(g):
            conv(q, g)

        if q == 0:
            sib_wait(1, *range(8))
        project(q)

    def group(k):
        return pl.ds(pl.multiple_of(16 * k, 16), 16)

    def forward(q):
        rows = pl.ds(2 * q, 2)
        for m in range(1, 8):
            k = (mine + m) % 8
            push(
                co.at[rows, group(k)], gbuf.at[rows, mine], asend.at[q, m - 1], arecv.at[q, m - 1], member(k)
            )
        gbuf[rows, mine] = co[rows, group(mine)]

    def arrived(q):
        rows = pl.ds(2 * q, 2)
        for m in range(1, 8):
            k = (mine + 8 - m) % 8
            ref = gbuf.at[rows, k]
            remote(ref, ref, asend.at[q, m - 1], arecv.at[q, m - 1], member(k)).wait_recv()

    lane = lax.broadcasted_iota(jnp.int32, (128, 128), 1)
    row = lax.broadcasted_iota(jnp.int32, (128, 128), 0)
    heads = [(lane // 32 == n) for n in range(4)]
    same = (lane // 8) % 2 == (row // 8) % 2
    same4 = jnp.concatenate([same] * 4, axis=0)

    def attend(q):
        held = gbuf[2 * q : 2 * q + 2].reshape(256, CH).astype(F32)
        center = jnp.mean(held, axis=-1, keepdims=True)
        off = held - center
        spread_of = jnp.mean(off * off, axis=-1, keepdims=True)
        ln = (off * lax.rsqrt(spread_of + 1e-05) * lng_ref[...] + lnb_ref[...]).astype(BF16)
        w = w2[:, 0:96].reshape(3 * CH, CH)
        qkv[:, 0:CH] = (dot_nt(ln, w[0:CH]) * Q_SCALE).astype(BF16)
        qkv[:, CH : 2 * CH] = dot_nt(ln, w[CH : 2 * CH]).astype(BF16)
        qkv[:, 2 * CH :] = dot_nt(ln, w[2 * CH :]).astype(BF16)

        @pl.loop(0, 2)
        def _(r):
            rows = pl.ds(pl.multiple_of(128 * r, 128), 128)
            parts = []
            for gr in range(4):
                lo = 128 * gr
                qv = qkv[rows, lo : lo + 128]
                kv = qkv[rows, CH + lo : CH + lo + 128]
                vv = qkv[rows, 2 * CH + lo : 2 * CH + lo + 128]
                zero = jnp.zeros_like(qv)
                qm = jnp.concatenate([jnp.where(m, qv, zero) for m in heads], axis=0)
                vm = jnp.concatenate([jnp.where(m, vv, zero) for m in heads], axis=0)
                e = jnp.where(same4, jnp.exp2(dot_nt(qm, kv)), 0.0)
                p = (e * (1.0 / jnp.sum(e, axis=1, keepdims=True))).astype(BF16)
                wide = jnp.concatenate([p[128 * n : 128 * (n + 1)] for n in range(4)], axis=1)
                parts.append(dot_nn(wide, vm).astype(BF16))
            done = dot_nt(jnp.concatenate(parts, axis=1), w2[:, 96:128].reshape(CH, CH))
            done = done + gbuf[2 * q + r].reshape(128, CH).astype(F32)
            fin[2 * q + r] = done.astype(BF16).reshape(8, 16, CH)

    def send_back(q):
        rows = pl.ds(2 * q, 2)
        for m in range(8):
            k = (mine + m) % 8
            src, dst = fin.at[rows, k], o_ref.at[rows, group(mine)]
            if m == 0:
                push_if(traded, src, dst, rsend.at[q, m], rrecv.at[q, m], owner(k))
                keep = pltpu.make_async_copy(src, dst, rrecv.at[q, m])
                pl.when(jnp.logical_not(traded))(keep.start)
            else:
                push(src, dst, rsend.at[q, m], rrecv.at[q, m], owner(k))

    def returned(q):
        rows = pl.ds(2 * q, 2)
        for m in range(8):
            ref = o_ref.at[rows, group((home + 8 - m) % 8)]
            remote(ref, ref, rsend.at[q, m], rrecv.at[q, m], dev_trade).wait_recv()

    mbconv(0)
    forward(0)
    g_finish(2, 1, 2, 3, 0)
    g_arrive(2, 4, 5, 6)
    expand(2)
    mbconv(1)
    forward(1)
    g_finish(2, 4, 5, 6)
    expand(3)
    sib_wait(2, *range(8))
    arrived(0)
    attend(0)
    send_back(0)
    expand_rim(1)
    mbconv(2)
    forward(2)
    arrived(1)
    attend(1)
    send_back(1)
    mbconv(3)
    forward(3)
    for q in range(2, 4):
        arrived(q)
        attend(q)
        send_back(q)
    for q in range(4):
        returned(q)
    for copy in pending:
        copy.wait_send()
    for cond, copy in guarded:
        pl.when(cond)(copy.wait_send)


def local(
    fields, bn_scale, bn_shift, w_expand, expand_bias, dw_kernel, dw_bias, w_project, ln_gain, ln_bias, w_qkv, w_out
):
    hbm = pl.BlockSpec(memory_space=pl.ANY)
    dma = pltpu.SemaphoreType.DMA
    out = pl.pallas_call(
        kernel,
        out_shape=jax.ShapeDtypeStruct((ROWS, COLS, CH), BF16),
        in_specs=[hbm] * 12,
        out_specs=hbm,
        scratch_shapes=[
            pltpu.VMEM((1, CH), F32),
            pltpu.VMEM((1, CH), F32),
            pltpu.VMEM((1, FF), F32),
            pltpu.VMEM((3, 3, FF), F32),
            pltpu.VMEM((1, FF), F32),
            pltpu.VMEM((1, CH), F32),
            pltpu.VMEM((1, CH), F32),
            pltpu.VMEM((ROWS, COLS, CH), BF16),
            pltpu.VMEM((2, COLS, CH), BF16),
            pltpu.VMEM((ROWS, COLS, CH), BF16),
            pltpu.VMEM((ROWS + 2, COLS, CH), BF16),
            pltpu.VMEM((16, CH, 128), BF16),
            pltpu.VMEM((16, 32, FF), BF16),
            pltpu.VMEM((16, 128, CH), BF16),
            pltpu.VMEM((16, ROWS + 2, 18, 8, 128), F32),
            pltpu.VMEM((8, 256, 256), BF16),
            pltpu.VMEM((ROWS, COLS, CH), BF16),
            pltpu.VMEM((ROWS, 8, 16, CH), BF16),
            pltpu.VMEM((256, 3 * CH), BF16),
            pltpu.VMEM((ROWS, 8, 16, CH), BF16),
            dma((11,)),
            dma((3, 29)),
            dma((3, 29)),
            dma((4,)),
            dma((4,)),
            dma((2,)),
            dma((2,)),
            dma((4, 7)),
            dma((4, 7)),
            dma((4, 8)),
            dma((4, 8)),
        ],
        compiler_params=pltpu.CompilerParams(
            collective_id=0, has_side_effects=True, vmem_limit_bytes=60 * 1024 * 1024
        ),
    )(
        fields.reshape(ROWS, COLS, CH),
        bn_scale.reshape(1, CH),
        bn_shift.reshape(1, CH),
        w_expand,
        expand_bias.reshape(1, FF),
        dw_kernel,
        dw_bias.reshape(1, FF),
        w_project.T,
        ln_gain.reshape(1, CH),
        ln_bias.reshape(1, CH),
        w_qkv.T,
        w_out.T,
    )
    return out.reshape(ROWS, 16, 8, CH).transpose(0, 2, 1, 3).reshape(fields.shape)


def solution(mesh):
    in_specs = (
        P("dp", "space", None, None),
        P(),
        P(),
        P(None, "dp"),
        P(),
        P(),
        P(),
        P(None, "dp"),
        P(),
        P(),
        P(None, "dp"),
        P(None, "dp"),
    )
    out_specs = P("dp", "space", None, None)
    return jax.shard_map(local, mesh=mesh, in_specs=in_specs, out_specs=out_specs, check_vma=False)
```

```python
import jax
import jax.numpy as jnp
from jax import lax
from jax.experimental import pallas as pl
from jax.experimental.pallas import tpu as pltpu
from jax.sharding import PartitionSpec as P

F32 = jnp.float32
BF16 = jnp.bfloat16
NY, NX, NZ = 4, 4, 4
ROWS, COLS, CH, FF = 8, 128, 512, 2048
Q_SCALE = 1.4426950408889634 / (32.0**0.5)
V_SCALE = 2.0**-10
TOP = float(jnp.finfo(jnp.bfloat16).max)


def dot_nn(a, b):
    return jnp.dot(a, b, preferred_element_type=F32)


def dot_nt(a, b):
    return lax.dot_general(a, b, (((1,), (1,)), ((), ())), preferred_element_type=F32)


def twice_gelu(x):
    return x + x * jnp.tanh(x * (0.7978845608028654 + 0.035677408136300125 * (x * x)))


def kernel(
    f_ref, bns_in, bnb_in, wex_ref, be_in, dwk_in, dwb_in, wpr_ref, lng_in, lnb_in, wqkv_ref, wout_ref,
    o_ref,
    bns_ref, bnb_ref, be_ref, dwk_ref, dwb_ref, lng_ref, lnb_ref,
    fbuf, halo, fperm, xn, we, w1, w2, ebuf, sbuf, co, gbuf, qkv, fin,
    lsem, wsend, wrecv, fsend, frecv, hsend, hrecv, asend, arecv, rsend, rrecv,
):
    dp = lax.axis_index("dp")
    sp = lax.axis_index("space")
    core, yy, zh = dp % 2, (dp // 2) % NY, dp // (2 * NY)
    xx, zl = sp // NZ, sp % NZ
    par, mine = zl // 2, 2 * xx + zl % 2
    band = 2 * mine + par
    home = sp // 2
    traded = (zl == 1) | (zl == 2)

    def at(z_hi, y, c, x, z_lo):
        return {"dp": (z_hi * NY + y) * 2 + c, "space": x * NZ + z_lo}

    y_up, y_dn, y_far = (yy + 1) % NY, (yy + NY - 1) % NY, (yy + 2) % NY
    dev_up = at(zh, y_up, core, xx, zl)
    dev_dn = at(zh, y_dn, core, xx, zl)
    dev_far = at(zh, y_far, core, xx, zl)
    dev_sib = at(zh, yy, 1 - core, xx, zl)
    dev_mir = at(1 - zh, yy, core, xx, NZ - 1 - zl)
    dev_xup = at(zh, yy, core, (xx + 1) % NX, zl)
    dev_xdn = at(zh, yy, core, (xx + NX - 1) % NX, zl)
    dev_trade = at(zh, yy, core, xx, NZ - 1 - zl)
    last_x, last_z = (xx + zl // 3) % NX, jnp.where(zl == 0, 2, jnp.where(zl == 2, 3, 0))
    first_x, first_z = jnp.where(zl == 0, xx + NX - 1, xx) % NX, jnp.where(zl == 0, 3, jnp.where(zl == 3, 1, 0))
    dev_last = at(zh, yy, core, last_x, last_z)
    dev_first = at(zh, yy, core, first_x, first_z)

    def member(k):
        return {"dp": dp, "space": (k // 2) * NZ + 2 * par + k % 2}

    def owner(k):
        return {"dp": dp, "space": 2 * k + par}

    barrier = pltpu.get_barrier_semaphore()
    peers = [dev_up, dev_dn, dev_far, dev_sib, dev_mir]
    peers += [{"dp": dp, "space": (sp + m) % 16} for m in range(1, 16)]
    for peer in peers:
        pl.semaphore_signal(barrier, inc=1, device_id=peer)

    pending = []

    def remote(src, dst, send, recv, dev):
        return pltpu.make_async_remote_copy(
            src_ref=src, dst_ref=dst, send_sem=send, recv_sem=recv, device_id=dev
        )

    def push(src, dst, send, recv, dev):
        copy = remote(src, dst, send, recv, dev)
        copy.start()
        pending.append(copy)

    guarded = []

    def push_if(cond, src, dst, send, recv, dev):
        copy = remote(src, dst, send, recv, dev)
        pl.when(cond)(copy.start)
        guarded.append((cond, copy))

    def shard(z_hi, y, c):
        return (z_hi * NY + y) * 2 + c

    own_d = shard(zh, yy, core)
    oth = 1 - zh
    bufs = (we, w1, w2)

    loads = [
        pltpu.make_async_copy(wex_ref, we.at[own_d], lsem.at[0]),
        pltpu.make_async_copy(wpr_ref, w1.at[own_d], lsem.at[1]),
        pltpu.make_async_copy(wqkv_ref, w2.at[own_d, 0:96], lsem.at[2]),
        pltpu.make_async_copy(wout_ref, w2.at[own_d, 96:128], lsem.at[3]),
    ]
    small = [
        (bns_in, bns_ref), (bnb_in, bnb_ref), (be_in, be_ref), (dwk_in, dwk_ref),
        (dwb_in, dwb_ref), (lng_in, lng_ref), (lnb_in, lnb_ref),
    ]
    loads += [pltpu.make_async_copy(src, dst, lsem.at[4 + n]) for n, (src, dst) in enumerate(small)]
    for load in loads:
        load.start()

    def pair(q):
        return pl.ds(2 * q, 2)

    stays = [(jnp.logical_not(traded), f_ref.at[pair(q)], fbuf.at[pair(q)], frecv.at[q]) for q in range(4)]
    stays += [(zl == 1, f_ref.at[ROWS - 1], halo.at[0], hrecv.at[0]), (zl == 2, f_ref.at[0], halo.at[1], hrecv.at[1])]
    for cond, src, dst, sem in stays:
        pl.when(cond)(pltpu.make_async_copy(src, dst, sem).start)
    pl.semaphore_wait(barrier, len(peers))

    odd = xx % 2
    unit = (128, 512, 32)

    def piece(ph, d, first, count):
        span = pl.ds(pl.multiple_of(first * unit[ph], unit[ph]), count * unit[ph])
        return bufs[ph].at[d, :, span] if ph == 1 else bufs[ph].at[d, span]

    places = [
        (oth, yy), (zh, y_dn), (zh, y_up), (zh, y_far), (oth, y_dn), (oth, y_up), (oth, y_far), (zh, yy)
    ]

    def wpush(ph, slot, ref, dev):
        push(ref, ref, wsend.at[ph, slot], wrecv.at[ph, slot], dev)

    def wwait(ph, slot, ref):
        remote(ref, ref, wsend.at[ph, slot], wrecv.at[ph, slot], dev_sib).wait_recv()

    def carried(ph, i):
        d = shard(*places[i], core)
        return bufs[ph].at[d] if ph == 2 else piece(ph, d, 2 * odd, 2)

    def spread(ph, i, base):
        ref = carried(ph, i)
        wpush(ph, base, ref, dev_up)
        wpush(ph, base + 1, ref, dev_dn)
        wpush(ph, base + 2, ref, dev_far)

    def g_start(ph):
        wpush(ph, 0, carried(ph, 7), dev_mir)
        spread(ph, 7, 1)
        wpush(ph, 21, bufs[ph].at[own_d], dev_sib)

    def g_arrive(ph, *which):
        for i in which:
            wwait(ph, i, carried(ph, i))
            if i == 0:
                spread(ph, 0, 4)
            d = shard(*places[i], core)
            if ph == 2:
                wpush(ph, 22 + i, bufs[ph].at[d], dev_sib)
                continue
            wpush(ph, 7 + 2 * i, piece(ph, d, 2 * odd, 1), dev_xup)
            wpush(ph, 8 + 2 * i, piece(ph, d, 2 * odd + 1, 1), dev_xdn)

    def g_finish(ph, *which):
        for i in which:
            d = shard(*places[i], core)
            wwait(ph, 7 + 2 * i, piece(ph, d, 2 - 2 * odd, 1))
            wwait(ph, 8 + 2 * i, piece(ph, d, 3 - 2 * odd, 1))
            wpush(ph, 22 + i, bufs[ph].at[d], dev_sib)

    def sib_wait(ph, *which):
        for i in which:
            slot = 21 if i == 7 else 22 + i
            wwait(ph, slot, bufs[ph].at[shard(*places[i], 1 - core)])

    loads[0].wait()
    g_start(0)
    push_if(zl != 1, f_ref.at[ROWS - 1], halo.at[0], hsend.at[0], hrecv.at[0], dev_last)
    for q in range(4):
        push_if(traded, f_ref.at[pair(q)], fbuf.at[pair(q)], fsend.at[q], frecv.at[q], dev_trade)
    push_if(zl != 2, f_ref.at[0], halo.at[1], hsend.at[1], hrecv.at[1], dev_first)
    loads[1].wait()
    g_start(1)

    tok = lax.broadcasted_iota(jnp.int32, (COLS, COLS), 0)
    col = lax.broadcasted_iota(jnp.int32, (COLS, COLS), 1)
    perm = ((tok % 8) * 16 + tok // 8 == col).astype(BF16)

    def prep(row, value):
        moved = dot_nn(perm, value)
        xn[row] = (moved * bns_ref[...] + bnb_ref[...]).astype(BF16)
        return moved.astype(BF16)

    def take(q):
        remote(fbuf.at[pair(q)], fbuf.at[pair(q)], fsend.at[q], frecv.at[q], dev_trade).wait_recv()
        for r in range(2 * q, 2 * q + 2):
            fperm[r] = prep(r + 1, fbuf[r])

    def expand_rows(first, count, *gs):
        rows = pl.ds(first, count)
        x = xn[rows].reshape(count * COLS, CH)
        sums = [dot_nn(x, jnp.concatenate([we[2 * g], we[2 * g + 1]], axis=1)) for g in gs]
        sub = lax.broadcasted_iota(jnp.int32, (count, 8, 128), 1)
        for g, summed in zip(gs, sums):
            e = twice_gelu(summed + be_ref[:, pl.ds(pl.multiple_of(256 * g, 256), 256)])
            for k in range(2):
                part = e[:, 128 * k : 128 * (k + 1)].reshape(count, 16, 8, 128)
                ebuf[2 * g + k, rows, 1:17] = part
                ebuf[2 * g + k, rows, 0] = jnp.where(sub == 0, 0.0, pltpu.roll(part[:, 15], 1, 1))
                ebuf[2 * g + k, rows, 17] = jnp.where(sub == 7, 0.0, pltpu.roll(part[:, 0], 7, 1))

    def early(*which):
        sib_wait(0, *which)
        for i in which:
            z_hi, y = places[i]

            @pl.loop(0, 2)
            def _(q):
                expand_rows(2 * q + 1, 2, z_hi * NY + y)

    def expand(q):
        take(q)

        @pl.loop(0, 4)
        def _(g):
            expand_rows(2 * q + 1, 2, 2 * g, 2 * g + 1)

    def expand_rim(side):
        remote(halo.at[side], halo.at[side], hsend.at[side], hrecv.at[side], dev_trade).wait_recv()
        at_row = (ROWS + 1) * side
        prep(at_row, halo[side])

        @pl.loop(0, 4)
        def _(g):
            expand_rows(at_row, 1, 2 * g, 2 * g + 1)

        @pl.when(band == 15 * side)
        def _():
            ebuf[:, at_row] = jnp.zeros((16, 18, 8, 128), F32)

    g_arrive(0, 1, 2, 3, 0)
    g_arrive(1, 1, 2, 3, 0)
    loads[2].wait()
    loads[3].wait()
    g_start(2)
    for load in loads[4:]:
        load.wait()
    dwk_ref[...] = 0.5 * dwk_ref[...]
    take(0)
    g_finish(0, 1, 2, 3, 0)
    g_arrive(0, 4, 5, 6)
    take(1)
    g_finish(1, 1, 2, 3, 0)
    early(7, 1)
    g_finish(0, 4, 5, 6)
    g_arrive(1, 4, 5, 6)
    early(2, 3, 0)
    g_arrive(2, 0)
    g_finish(1, 4, 5, 6)
    early(4, 5, 6)
    g_arrive(2, 1, 2, 3)
    expand_rim(0)

    def conv(q, g):
        for k in range(2):
            lanes = pl.ds(pl.multiple_of(256 * g + 128 * k, 128), 128)
            bias = dwb_ref[:, lanes]
            for r in range(2):
                summed = jnp.broadcast_to(bias[None], (16, 8, 128))
                for i in range(3):
                    for j in range(3):
                        tap = dwk_ref[i, j : j + 1, lanes]
                        summed = summed + ebuf[2 * g + k, 2 * q + r + i, j : j + 16] * tap[None]
                sbuf[g, 128 * r : 128 * (r + 1), 128 * k : 128 * (k + 1)] = (
                    twice_gelu(summed).astype(BF16).reshape(128, 128)
                )

    def project(q):
        w = w1[...].reshape(CH, FF)
        total = dot_nt(sbuf[0], w[:, 0:256])
        for g in range(1, 8):
            total = total + dot_nt(sbuf[g], w[:, 256 * g : 256 * (g + 1)])
        total = 0.5 * total + fperm[2 * q : 2 * q + 2].reshape(2 * COLS, CH).astype(F32)
        co[2 * q : 2 * q + 2] = total.astype(BF16).reshape(2, COLS, CH)

    def mbconv(q):
        @pl.loop(0, 8)
        def _(g):
            conv(q, g)

        if q == 0:
            sib_wait(1, *range(8))
        project(q)

    def group(k):
        return pl.ds(pl.multiple_of(16 * k, 16), 16)

    def forward(q):
        rows = pl.ds(2 * q, 2)
        for m in range(1, 8):
            k = (mine + m) % 8
            push(
                co.at[rows, group(k)], gbuf.at[rows, mine], asend.at[q, m - 1], arecv.at[q, m - 1], member(k)
            )
        gbuf[rows, mine] = co[rows, group(mine)]

    def arrived(q):
        rows = pl.ds(2 * q, 2)
        for m in range(1, 8):
            k = (mine + 8 - m) % 8
            ref = gbuf.at[rows, k]
            remote(ref, ref, asend.at[q, m - 1], arecv.at[q, m - 1], member(k)).wait_recv()

    lane = lax.broadcasted_iota(jnp.int32, (128, 128), 1)
    row = lax.broadcasted_iota(jnp.int32, (128, 128), 0)
    heads = [(lane // 32 == n) for n in range(4)]
    same = (lane // 8) % 2 == (row // 8) % 2
    same4 = jnp.concatenate([same] * 4, axis=0)
    ones = jnp.concatenate([m.astype(BF16) for m in heads], axis=0)

    def attend(q):
        held = gbuf[2 * q : 2 * q + 2].reshape(256, CH).astype(F32)
        center = jnp.mean(held, axis=-1, keepdims=True)
        off = held - center
        spread_of = jnp.mean(off * off, axis=-1, keepdims=True)
        ln = (off * lax.rsqrt(spread_of + 1e-05) * lng_ref[...] + lnb_ref[...]).astype(BF16)
        w = w2[:, 0:96].reshape(3 * CH, CH)
        qkv[:, 0:CH] = (dot_nt(ln, w[0:CH]) * Q_SCALE).astype(BF16)
        qkv[:, CH : 2 * CH] = dot_nt(ln, w[CH : 2 * CH]).astype(BF16)
        qkv[:, 2 * CH :] = (dot_nt(ln, w[2 * CH :]) * V_SCALE).astype(BF16)

        for r in range(2):
            parts = []
            for gr in range(4):
                lo = 128 * gr
                rows = slice(128 * r, 128 * (r + 1))
                qv = qkv[rows, lo : lo + 128]
                kv = qkv[rows, CH + lo : CH + lo + 128]
                vv = qkv[rows, 2 * CH + lo : 2 * CH + lo + 128]
                zero = jnp.zeros_like(qv)
                qm = jnp.concatenate([jnp.where(m, qv, zero) for m in heads], axis=0)
                vm = jnp.concatenate([jnp.where(m, vv, zero) for m in heads], axis=0)
                e = jnp.where(same4, jnp.minimum(jnp.exp2(dot_nt(qm, kv)), TOP), 0.0).astype(BF16)
                wide = jnp.concatenate([e[128 * n : 128 * (n + 1)] for n in range(4)], axis=1)
                both = dot_nn(wide, jnp.concatenate([vm, ones], axis=1))
                parts.append((both[:, 0:128] * (1.0 / both[:, 128:]) * (1.0 / V_SCALE)).astype(BF16))
            done = dot_nt(jnp.concatenate(parts, axis=1), w2[:, 96:128].reshape(CH, CH))
            done = done + gbuf[2 * q + r].reshape(128, CH).astype(F32)
            fin[2 * q + r] = done.astype(BF16).reshape(8, 16, CH)
            send_back(2 * q + r)

    def send_back(r):
        for m in range(8):
            k = (mine + m) % 8
            src, dst = fin.at[r, k], o_ref.at[r, group(mine)]
            if m == 0:
                push_if(traded, src, dst, rsend.at[r, m], rrecv.at[r, m], owner(k))
                keep = pltpu.make_async_copy(src, dst, rrecv.at[r, m])
                pl.when(jnp.logical_not(traded))(keep.start)
            else:
                push(src, dst, rsend.at[r, m], rrecv.at[r, m], owner(k))

    def returned(r):
        for m in range(8):
            ref = o_ref.at[r, group((home + 8 - m) % 8)]
            remote(ref, ref, rsend.at[r, m], rrecv.at[r, m], dev_trade).wait_recv()

    mbconv(0)
    forward(0)
    expand(2)
    g_arrive(2, 4, 5, 6)
    mbconv(1)
    forward(1)
    sib_wait(2, *range(8))
    arrived(0)
    attend(0)
    expand(3)
    mbconv(2)
    forward(2)
    arrived(1)
    attend(1)
    expand_rim(1)
    mbconv(3)
    forward(3)
    for q in range(2, 4):
        arrived(q)
        attend(q)
    for r in range(ROWS):
        returned(r)
    for copy in pending:
        copy.wait_send()
    for cond, copy in guarded:
        pl.when(cond)(copy.wait_send)


def local(
    fields, bn_scale, bn_shift, w_expand, expand_bias, dw_kernel, dw_bias, w_project, ln_gain, ln_bias, w_qkv, w_out
):
    hbm = pl.BlockSpec(memory_space=pl.ANY)
    dma = pltpu.SemaphoreType.DMA
    out = pl.pallas_call(
        kernel,
        out_shape=jax.ShapeDtypeStruct((ROWS, COLS, CH), BF16),
        in_specs=[hbm] * 12,
        out_specs=hbm,
        scratch_shapes=[
            pltpu.VMEM((1, CH), F32),
            pltpu.VMEM((1, CH), F32),
            pltpu.VMEM((1, FF), F32),
            pltpu.VMEM((3, 3, FF), F32),
            pltpu.VMEM((1, FF), F32),
            pltpu.VMEM((1, CH), F32),
            pltpu.VMEM((1, CH), F32),
            pltpu.VMEM((ROWS, COLS, CH), BF16),
            pltpu.VMEM((2, COLS, CH), BF16),
            pltpu.VMEM((ROWS, COLS, CH), BF16),
            pltpu.VMEM((ROWS + 2, COLS, CH), BF16),
            pltpu.VMEM((16, CH, 128), BF16),
            pltpu.VMEM((16, 32, FF), BF16),
            pltpu.VMEM((16, 128, CH), BF16),
            pltpu.VMEM((16, ROWS + 2, 18, 8, 128), F32),
            pltpu.VMEM((8, 256, 256), BF16),
            pltpu.VMEM((ROWS, COLS, CH), BF16),
            pltpu.VMEM((ROWS, 8, 16, CH), BF16),
            pltpu.VMEM((256, 3 * CH), BF16),
            pltpu.VMEM((ROWS, 8, 16, CH), BF16),
            dma((11,)),
            dma((3, 29)),
            dma((3, 29)),
            dma((4,)),
            dma((4,)),
            dma((2,)),
            dma((2,)),
            dma((4, 7)),
            dma((4, 7)),
            dma((ROWS, 8)),
            dma((ROWS, 8)),
        ],
        compiler_params=pltpu.CompilerParams(
            collective_id=0, has_side_effects=True, vmem_limit_bytes=60 * 1024 * 1024
        ),
    )(
        fields.reshape(ROWS, COLS, CH),
        bn_scale.reshape(1, CH),
        bn_shift.reshape(1, CH),
        w_expand,
        expand_bias.reshape(1, FF),
        dw_kernel,
        dw_bias.reshape(1, FF),
        w_project.T,
        ln_gain.reshape(1, CH),
        ln_bias.reshape(1, CH),
        w_qkv.T,
        w_out.T,
    )
    return out.reshape(ROWS, 16, 8, CH).transpose(0, 2, 1, 3).reshape(fields.shape)


def solution(mesh):
    in_specs = (
        P("dp", "space", None, None),
        P(),
        P(),
        P(None, "dp"),
        P(),
        P(),
        P(),
        P(None, "dp"),
        P(),
        P(),
        P(None, "dp"),
        P(None, "dp"),
    )
    out_specs = P("dp", "space", None, None)
    return jax.shard_map(local, mesh=mesh, in_specs=in_specs, out_specs=out_specs, check_vma=False)
```

```python
import jax
import jax.numpy as jnp
from jax import lax
from jax.experimental import pallas as pl
from jax.experimental.pallas import tpu as pltpu
from jax.sharding import PartitionSpec as P

F32 = jnp.float32
BF16 = jnp.bfloat16
NY, NX, NZ = 4, 4, 4
ROWS, COLS, CH, FF = 8, 128, 512, 2048
Q_SCALE = 1.4426950408889634 / (32.0**0.5)
V_SCALE = 2.0**-10
TOP = float(jnp.finfo(jnp.bfloat16).max)


def dot_nn(a, b):
    return jnp.dot(a, b, preferred_element_type=F32)


def dot_nt(a, b):
    return lax.dot_general(a, b, (((1,), (1,)), ((), ())), preferred_element_type=F32)


def twice_gelu(x):
    return x + x * jnp.tanh(x * (0.7978845608028654 + 0.035677408136300125 * (x * x)))


def kernel(
    f_ref, bns_in, bnb_in, wex_ref, be_in, dwk_in, dwb_in, wpr_ref, lng_in, lnb_in, wqkv_ref, wout_ref,
    o_ref,
    bns_ref, bnb_ref, be_ref, dwk_ref, dwb_ref, lng_ref, lnb_ref,
    fbuf, halo, fperm, xn, we, w1, w2, ebuf, sbuf, co, gbuf, qkv, fin,
    lsem, wsend, wrecv, fsend, frecv, hsend, hrecv, asend, arecv, rsend, rrecv,
):
    dp = lax.axis_index("dp")
    sp = lax.axis_index("space")
    core, yy, zh = dp % 2, (dp // 2) % NY, dp // (2 * NY)
    xx, zl = sp // NZ, sp % NZ
    par, mine = zl // 2, 2 * xx + zl % 2
    band = 2 * mine + par
    home = sp // 2
    traded = (zl == 1) | (zl == 2)

    def at(z_hi, y, c, x, z_lo):
        return {"dp": (z_hi * NY + y) * 2 + c, "space": x * NZ + z_lo}

    y_up, y_dn, y_far = (yy + 1) % NY, (yy + NY - 1) % NY, (yy + 2) % NY
    dev_up = at(zh, y_up, core, xx, zl)
    dev_dn = at(zh, y_dn, core, xx, zl)
    dev_far = at(zh, y_far, core, xx, zl)
    dev_sib = at(zh, yy, 1 - core, xx, zl)
    dev_mir = at(1 - zh, yy, core, xx, NZ - 1 - zl)
    dev_xup = at(zh, yy, core, (xx + 1) % NX, zl)
    dev_xdn = at(zh, yy, core, (xx + NX - 1) % NX, zl)
    dev_trade = at(zh, yy, core, xx, NZ - 1 - zl)
    last_x, last_z = (xx + zl // 3) % NX, jnp.where(zl == 0, 2, jnp.where(zl == 2, 3, 0))
    first_x, first_z = jnp.where(zl == 0, xx + NX - 1, xx) % NX, jnp.where(zl == 0, 3, jnp.where(zl == 3, 1, 0))
    dev_last = at(zh, yy, core, last_x, last_z)
    dev_first = at(zh, yy, core, first_x, first_z)

    def member(k):
        return {"dp": dp, "space": (k // 2) * NZ + 2 * par + k % 2}

    def owner(k):
        return {"dp": dp, "space": 2 * k + par}

    barrier = pltpu.get_barrier_semaphore()
    peers = [dev_up, dev_dn, dev_far, dev_sib, dev_mir]
    peers += [{"dp": dp, "space": (sp + m) % 16} for m in range(1, 16)]
    for peer in peers:
        pl.semaphore_signal(barrier, inc=1, device_id=peer)

    pending = []

    def remote(src, dst, send, recv, dev):
        return pltpu.make_async_remote_copy(
            src_ref=src, dst_ref=dst, send_sem=send, recv_sem=recv, device_id=dev
        )

    def push(src, dst, send, recv, dev):
        copy = remote(src, dst, send, recv, dev)
        copy.start()
        pending.append(copy)

    guarded = []

    def push_if(cond, src, dst, send, recv, dev):
        copy = remote(src, dst, send, recv, dev)
        pl.when(cond)(copy.start)
        guarded.append((cond, copy))

    def shard(z_hi, y, c):
        return (z_hi * NY + y) * 2 + c

    own_d = shard(zh, yy, core)
    oth = 1 - zh
    bufs = (we, w1, w2)

    loads = [
        pltpu.make_async_copy(wex_ref, we.at[own_d], lsem.at[0]),
        pltpu.make_async_copy(wpr_ref, w1.at[own_d], lsem.at[1]),
        pltpu.make_async_copy(wqkv_ref, w2.at[own_d, 0:96], lsem.at[2]),
        pltpu.make_async_copy(wout_ref, w2.at[own_d, 96:128], lsem.at[3]),
    ]
    small = [
        (bns_in, bns_ref), (bnb_in, bnb_ref), (be_in, be_ref), (dwk_in, dwk_ref),
        (dwb_in, dwb_ref), (lng_in, lng_ref), (lnb_in, lnb_ref),
    ]
    loads += [pltpu.make_async_copy(src, dst, lsem.at[4 + n]) for n, (src, dst) in enumerate(small)]
    for load in loads:
        load.start()

    def pair(q):
        return pl.ds(2 * q, 2)

    stays = [(jnp.logical_not(traded), f_ref.at[pair(q)], fbuf.at[pair(q)], frecv.at[q]) for q in range(4)]
    stays += [(zl == 1, f_ref.at[ROWS - 1], halo.at[0], hrecv.at[0]), (zl == 2, f_ref.at[0], halo.at[1], hrecv.at[1])]
    for cond, src, dst, sem in stays:
        pl.when(cond)(pltpu.make_async_copy(src, dst, sem).start)
    pl.semaphore_wait(barrier, len(peers))

    odd = xx % 2
    unit = (128, 512, 32)

    def piece(ph, d, first, count):
        span = pl.ds(pl.multiple_of(first * unit[ph], unit[ph]), count * unit[ph])
        return bufs[ph].at[d, :, span] if ph == 1 else bufs[ph].at[d, span]

    places = [
        (oth, yy), (zh, y_dn), (zh, y_up), (zh, y_far), (oth, y_dn), (oth, y_up), (oth, y_far), (zh, yy)
    ]

    def wpush(ph, slot, ref, dev):
        push(ref, ref, wsend.at[ph, slot], wrecv.at[ph, slot], dev)

    def wwait(ph, slot, ref):
        remote(ref, ref, wsend.at[ph, slot], wrecv.at[ph, slot], dev_sib).wait_recv()

    def carried(ph, i):
        d = shard(*places[i], core)
        return bufs[ph].at[d] if ph == 2 else piece(ph, d, 2 * odd, 2)

    def spread(ph, i, base):
        ref = carried(ph, i)
        wpush(ph, base, ref, dev_up)
        wpush(ph, base + 1, ref, dev_dn)
        wpush(ph, base + 2, ref, dev_far)

    def g_start(ph):
        wpush(ph, 0, carried(ph, 7), dev_mir)
        spread(ph, 7, 1)
        wpush(ph, 21, bufs[ph].at[own_d], dev_sib)

    def g_arrive(ph, *which):
        for i in which:
            wwait(ph, i, carried(ph, i))
            if i == 0:
                spread(ph, 0, 4)
            d = shard(*places[i], core)
            if ph == 2:
                wpush(ph, 22 + i, bufs[ph].at[d], dev_sib)
                continue
            wpush(ph, 7 + 2 * i, piece(ph, d, 2 * odd, 1), dev_xup)
            wpush(ph, 8 + 2 * i, piece(ph, d, 2 * odd + 1, 1), dev_xdn)

    def g_finish(ph, *which):
        for i in which:
            d = shard(*places[i], core)
            wwait(ph, 7 + 2 * i, piece(ph, d, 2 - 2 * odd, 1))
            wwait(ph, 8 + 2 * i, piece(ph, d, 3 - 2 * odd, 1))
            wpush(ph, 22 + i, bufs[ph].at[d], dev_sib)

    def sib_wait(ph, *which):
        for i in which:
            slot = 21 if i == 7 else 22 + i
            wwait(ph, slot, bufs[ph].at[shard(*places[i], 1 - core)])

    loads[0].wait()
    g_start(0)
    push_if(zl != 1, f_ref.at[ROWS - 1], halo.at[0], hsend.at[0], hrecv.at[0], dev_last)
    for q in range(4):
        push_if(traded, f_ref.at[pair(q)], fbuf.at[pair(q)], fsend.at[q], frecv.at[q], dev_trade)
    push_if(zl != 2, f_ref.at[0], halo.at[1], hsend.at[1], hrecv.at[1], dev_first)
    loads[1].wait()
    g_start(1)

    tok = lax.broadcasted_iota(jnp.int32, (COLS, COLS), 0)
    col = lax.broadcasted_iota(jnp.int32, (COLS, COLS), 1)
    perm = ((tok % 8) * 16 + tok // 8 == col).astype(BF16)

    def prep(row, value):
        moved = dot_nn(perm, value)
        xn[row] = (moved * bns_ref[...] + bnb_ref[...]).astype(BF16)
        return moved.astype(BF16)

    def take(q):
        remote(fbuf.at[pair(q)], fbuf.at[pair(q)], fsend.at[q], frecv.at[q], dev_trade).wait_recv()
        for r in range(2 * q, 2 * q + 2):
            fperm[r] = prep(r + 1, fbuf[r])

    def expand_rows(first, count, *gs):
        rows = pl.ds(first, count)
        x = xn[rows].reshape(count * COLS, CH)
        sums = [dot_nn(x, jnp.concatenate([we[2 * g], we[2 * g + 1]], axis=1)) for g in gs]
        sub = lax.broadcasted_iota(jnp.int32, (count, 8, 128), 1)
        for g, summed in zip(gs, sums):
            e = twice_gelu(summed + be_ref[:, pl.ds(pl.multiple_of(256 * g, 256), 256)])
            for k in range(2):
                part = e[:, 128 * k : 128 * (k + 1)].reshape(count, 16, 8, 128)
                ebuf[2 * g + k, rows, 1:17] = part
                ebuf[2 * g + k, rows, 0] = jnp.where(sub == 0, 0.0, pltpu.roll(part[:, 15], 1, 1))
                ebuf[2 * g + k, rows, 17] = jnp.where(sub == 7, 0.0, pltpu.roll(part[:, 0], 7, 1))

    def early(*which):
        sib_wait(0, *which)
        for i in which:
            z_hi, y = places[i]

            @pl.loop(0, 2)
            def _(q):
                expand_rows(2 * q + 1, 2, z_hi * NY + y)

    def expand(q):
        take(q)

        @pl.loop(0, 4)
        def _(g):
            expand_rows(2 * q + 1, 2, 2 * g, 2 * g + 1)

    def expand_rim(side):
        remote(halo.at[side], halo.at[side], hsend.at[side], hrecv.at[side], dev_trade).wait_recv()
        at_row = (ROWS + 1) * side
        prep(at_row, halo[side])

        @pl.loop(0, 4)
        def _(g):
            expand_rows(at_row, 1, 2 * g, 2 * g + 1)

        @pl.when(band == 15 * side)
        def _():
            ebuf[:, at_row] = jnp.zeros((16, 18, 8, 128), F32)

    g_arrive(0, 1, 2, 3, 0)
    g_arrive(1, 1, 2, 3, 0)
    loads[2].wait()
    loads[3].wait()
    g_start(2)
    for load in loads[4:]:
        load.wait()
    dwk_ref[...] = 0.5 * dwk_ref[...]
    take(0)
    g_finish(0, 1, 2, 3, 0)
    g_arrive(0, 4, 5, 6)
    g_finish(1, 1, 2, 3, 0)
    g_finish(0, 4, 5, 6)
    g_arrive(1, 4, 5, 6)
    take(1)
    early(7, 1, 2, 3, 0)
    g_arrive(2, 0)
    g_finish(1, 4, 5, 6)
    early(4, 5, 6)
    g_arrive(2, 1, 2, 3)
    expand_rim(0)

    def conv(q, g):
        for k in range(2):
            lanes = pl.ds(pl.multiple_of(256 * g + 128 * k, 128), 128)
            bias = dwb_ref[:, lanes]
            for r in range(2):
                summed = jnp.broadcast_to(bias[None], (16, 8, 128))
                for i in range(3):
                    for j in range(3):
                        tap = dwk_ref[i, j : j + 1, lanes]
                        summed = summed + ebuf[2 * g + k, 2 * q + r + i, j : j + 16] * tap[None]
                sbuf[g, 128 * r : 128 * (r + 1), 128 * k : 128 * (k + 1)] = (
                    twice_gelu(summed).astype(BF16).reshape(128, 128)
                )

    def project(q):
        w = w1[...].reshape(CH, FF)
        total = dot_nt(sbuf[0], w[:, 0:256])
        for g in range(1, 8):
            total = total + dot_nt(sbuf[g], w[:, 256 * g : 256 * (g + 1)])
        total = 0.5 * total + fperm[2 * q : 2 * q + 2].reshape(2 * COLS, CH).astype(F32)
        co[2 * q : 2 * q + 2] = total.astype(BF16).reshape(2, COLS, CH)

    def mbconv(q):
        @pl.loop(0, 8)
        def _(g):
            conv(q, g)

        if q == 0:
            sib_wait(1, *range(8))
        project(q)

    def group(k):
        return pl.ds(pl.multiple_of(16 * k, 16), 16)

    def forward(q):
        rows = pl.ds(2 * q, 2)
        for m in range(1, 8):
            k = (mine + m) % 8
            push(
                co.at[rows, group(k)], gbuf.at[rows, mine], asend.at[q, m - 1], arecv.at[q, m - 1], member(k)
            )
        gbuf[rows, mine] = co[rows, group(mine)]

    def arrived(q):
        rows = pl.ds(2 * q, 2)
        for m in range(1, 8):
            k = (mine + 8 - m) % 8
            ref = gbuf.at[rows, k]
            remote(ref, ref, asend.at[q, m - 1], arecv.at[q, m - 1], member(k)).wait_recv()

    lane = lax.broadcasted_iota(jnp.int32, (128, 128), 1)
    row = lax.broadcasted_iota(jnp.int32, (128, 128), 0)
    heads = [(lane // 32 == n) for n in range(4)]
    same = (lane // 8) % 2 == (row // 8) % 2
    same4 = jnp.concatenate([same] * 4, axis=0)
    ones = jnp.concatenate([m.astype(BF16) for m in heads], axis=0)

    def attend(q):
        held = gbuf[2 * q : 2 * q + 2].reshape(256, CH).astype(F32)
        center = jnp.mean(held, axis=-1, keepdims=True)
        off = held - center
        spread_of = jnp.mean(off * off, axis=-1, keepdims=True)
        ln = (off * lax.rsqrt(spread_of + 1e-05) * lng_ref[...] + lnb_ref[...]).astype(BF16)
        w = w2[:, 0:96].reshape(3 * CH, CH)
        qkv[:, 0:CH] = (dot_nt(ln, w[0:CH]) * Q_SCALE).astype(BF16)
        qkv[:, CH : 2 * CH] = dot_nt(ln, w[CH : 2 * CH]).astype(BF16)
        qkv[:, 2 * CH :] = (dot_nt(ln, w[2 * CH :]) * V_SCALE).astype(BF16)

        for r in range(2):
            parts = []
            for gr in range(4):
                lo = 128 * gr
                rows = slice(128 * r, 128 * (r + 1))
                qv = qkv[rows, lo : lo + 128]
                kv = qkv[rows, CH + lo : CH + lo + 128]
                vv = qkv[rows, 2 * CH + lo : 2 * CH + lo + 128]
                zero = jnp.zeros_like(qv)
                qm = jnp.concatenate([jnp.where(m, qv, zero) for m in heads], axis=0)
                vm = jnp.concatenate([jnp.where(m, vv, zero) for m in heads], axis=0)
                e = jnp.where(same4, jnp.minimum(jnp.exp2(dot_nt(qm, kv)), TOP), 0.0).astype(BF16)
                wide = jnp.concatenate([e[128 * n : 128 * (n + 1)] for n in range(4)], axis=1)
                both = dot_nn(wide, jnp.concatenate([vm, ones], axis=1))
                parts.append((both[:, 0:128] * (1.0 / both[:, 128:]) * (1.0 / V_SCALE)).astype(BF16))
            done = dot_nt(jnp.concatenate(parts, axis=1), w2[:, 96:128].reshape(CH, CH))
            done = done + gbuf[2 * q + r].reshape(128, CH).astype(F32)
            fin[2 * q + r] = done.astype(BF16).reshape(8, 16, CH)
            send_back(2 * q + r)

    def send_back(r):
        for m in range(8):
            k = (mine + m) % 8
            src, dst = fin.at[r, k], o_ref.at[r, group(mine)]
            if m == 0:
                push_if(traded, src, dst, rsend.at[r, m], rrecv.at[r, m], owner(k))
                keep = pltpu.make_async_copy(src, dst, rrecv.at[r, m])
                pl.when(jnp.logical_not(traded))(keep.start)
            else:
                push(src, dst, rsend.at[r, m], rrecv.at[r, m], owner(k))

    def returned(r):
        for m in range(8):
            ref = o_ref.at[r, group((home + 8 - m) % 8)]
            remote(ref, ref, rsend.at[r, m], rrecv.at[r, m], dev_trade).wait_recv()

    mbconv(0)
    forward(0)
    expand(2)
    g_arrive(2, 4, 5, 6)
    mbconv(1)
    forward(1)
    sib_wait(2, *range(8))
    arrived(0)
    attend(0)
    expand(3)
    mbconv(2)
    forward(2)
    arrived(1)
    attend(1)
    expand_rim(1)
    mbconv(3)
    forward(3)
    for q in range(2, 4):
        arrived(q)
        attend(q)
    for r in range(ROWS):
        returned(r)
    for copy in pending:
        copy.wait_send()
    for cond, copy in guarded:
        pl.when(cond)(copy.wait_send)


def local(
    fields, bn_scale, bn_shift, w_expand, expand_bias, dw_kernel, dw_bias, w_project, ln_gain, ln_bias, w_qkv, w_out
):
    hbm = pl.BlockSpec(memory_space=pl.ANY)
    dma = pltpu.SemaphoreType.DMA
    out = pl.pallas_call(
        kernel,
        out_shape=jax.ShapeDtypeStruct((ROWS, COLS, CH), BF16),
        in_specs=[hbm] * 12,
        out_specs=hbm,
        scratch_shapes=[
            pltpu.VMEM((1, CH), F32),
            pltpu.VMEM((1, CH), F32),
            pltpu.VMEM((1, FF), F32),
            pltpu.VMEM((3, 3, FF), F32),
            pltpu.VMEM((1, FF), F32),
            pltpu.VMEM((1, CH), F32),
            pltpu.VMEM((1, CH), F32),
            pltpu.VMEM((ROWS, COLS, CH), BF16),
            pltpu.VMEM((2, COLS, CH), BF16),
            pltpu.VMEM((ROWS, COLS, CH), BF16),
            pltpu.VMEM((ROWS + 2, COLS, CH), BF16),
            pltpu.VMEM((16, CH, 128), BF16),
            pltpu.VMEM((16, 32, FF), BF16),
            pltpu.VMEM((16, 128, CH), BF16),
            pltpu.VMEM((16, ROWS + 2, 18, 8, 128), F32),
            pltpu.VMEM((8, 256, 256), BF16),
            pltpu.VMEM((ROWS, COLS, CH), BF16),
            pltpu.VMEM((ROWS, 8, 16, CH), BF16),
            pltpu.VMEM((256, 3 * CH), BF16),
            pltpu.VMEM((ROWS, 8, 16, CH), BF16),
            dma((11,)),
            dma((3, 29)),
            dma((3, 29)),
            dma((4,)),
            dma((4,)),
            dma((2,)),
            dma((2,)),
            dma((4, 7)),
            dma((4, 7)),
            dma((ROWS, 8)),
            dma((ROWS, 8)),
        ],
        compiler_params=pltpu.CompilerParams(
            collective_id=0, has_side_effects=True, vmem_limit_bytes=60 * 1024 * 1024
        ),
    )(
        fields.reshape(ROWS, COLS, CH),
        bn_scale.reshape(1, CH),
        bn_shift.reshape(1, CH),
        w_expand,
        expand_bias.reshape(1, FF),
        dw_kernel,
        dw_bias.reshape(1, FF),
        w_project.T,
        ln_gain.reshape(1, CH),
        ln_bias.reshape(1, CH),
        w_qkv.T,
        w_out.T,
    )
    return out.reshape(ROWS, 16, 8, CH).transpose(0, 2, 1, 3).reshape(fields.shape)


def solution(mesh):
    in_specs = (
        P("dp", "space", None, None),
        P(),
        P(),
        P(None, "dp"),
        P(),
        P(),
        P(),
        P(None, "dp"),
        P(),
        P(),
        P(None, "dp"),
        P(None, "dp"),
    )
    out_specs = P("dp", "space", None, None)
    return jax.shard_map(local, mesh=mesh, in_specs=in_specs, out_specs=out_specs, check_vma=False)
```
